32 devices in a mesh: tile: 16 (over z, x, core), chan: 2 (over y).
Axes of the slice: x: 2, y: 2, z: 4, core: 2. Of those that a mesh axis runs over, the one named last changes fastest.
Arguments:
- x_slab: bfloat16 [16, 96, 6, 8, 256], P('tile', 'chan'), may hold values from -6 to 6
- weights: bfloat16 [96, 96, 27], P(None, 'chan'), may hold values from -0.125 to 0.125
- cotangent: bfloat16 [16, 96, 4, 8, 256], P('tile', 'chan'), may hold values from -6 to 6
Outputs:
- out_field: bfloat16 [16, 96, 4, 8, 256], P('tile', 'chan')
- in_grad: bfloat16 [16, 96, 6, 8, 256], P('tile', 'chan')
- weight_grad: float32 [96, 96, 27], P(None, 'chan')
The draws below stay inside these ranges and needn't reach their ends.
All inputs are finite; a program needn't handle non-finite values.
Results may differ from the reference program's by a relative error of at most 0.001.
Values may be sent and summed in bfloat16 or wider, within the bound.
A program may use at most 320 MiB of HBM per device.

```python
import math
import jax
import jax.numpy as jnp
from jax import lax

CH = 96
ZP = 4
TY = 8
TX = 256
TILES = 16
NY = 128
NX = 256


def level_of(key, shape, cuts, low, largest):
    level = 1.0
    for position, shards_of in cuts:
        steps = jax.random.uniform(jax.random.fold_in(jax.random.fold_in(key, 6), position), (shards_of,), jnp.float32, low / len(cuts), largest / len(cuts))
        level = level * jnp.repeat(jnp.exp(steps), shape[position] // shards_of).reshape((-1,) + (1,) * (len(shape) - 1 - position))
    return level


def bell_draw(rng, shape, scale, limit, shards=(), dtype=jnp.bfloat16):
    entries = jax.random.normal(rng, shape, jnp.float32) * scale
    if len(shards) > 0:
        entries = level_of(rng, shape, shards, -0.22, 0.18) * entries
    return jnp.clip(entries, min=-limit, max=limit).astype(dtype)


def setup_inputs(seed: int = 0) -> dict:
    keys = jax.random.split(jax.random.key(seed), 4)
    return {
        "x_slab": bell_draw(keys[0], (TILES, CH, ZP + 2, TY, TX), 1.0, 6.0, ((0, 16), (1, 2))),
        "weights": bell_draw(keys[1], (CH, CH, 27), (CH * 27) ** -0.5, 0.125, ((1, 2),)),
        "cotangent": bell_draw(keys[2], (TILES, CH, ZP, TY, TX), 1.0, 6.0, ((0, 16), (1, 2))),
    }


def to_planes(blocks):
    count, chans, planes, height, width = blocks.shape
    return blocks.transpose(1, 2, 0, 3, 4).reshape(chans, planes, count * height, width)

def to_blocks(field):
    chans, planes, height_all, width_all = field.shape
    strips = height_all // TY
    return field.reshape(chans, planes, strips, TY, width_all).transpose(2, 0, 1, 3, 4)

def reference(x_slab, weights, cotangent):
    field = to_planes(x_slab).astype(jnp.float32)
    grads_out = to_planes(cotangent).astype(jnp.float32)
    kernel = weights.astype(jnp.float32)
    padded = jnp.pad(field, ((0, 0), (0, 0), (1, 1), (1, 1)))
    grad_flat = grads_out.reshape(CH, ZP * NY * NX)
    total = jnp.zeros((CH, ZP * NY * NX), jnp.float32)
    kernel_terms = []
    for tap in range(27):
        deep_off, row_off, col_off = (tap // 9, tap // 3 % 3, tap % 3)
        shifted = padded[:, deep_off:deep_off + ZP, row_off:row_off + NY, col_off:col_off + NX].reshape(CH, ZP * NY * NX)
        total = total + jnp.dot(kernel[:, :, tap], shifted, precision=lax.Precision.HIGHEST)
        kernel_terms.append(jnp.dot(grad_flat, shifted.T, precision=lax.Precision.HIGHEST))
    grad_pad = jnp.pad(grads_out, ((0, 0), (2, 2), (1, 1), (1, 1)))
    back = jnp.zeros((CH, (ZP + 2) * NY * NX), jnp.float32)
    for tap in range(27):
        deep_off, row_off, col_off = (tap // 9, tap // 3 % 3, tap % 3)
        window = grad_pad[:, 2 - deep_off:4 - deep_off + ZP, 2 - row_off:2 - row_off + NY, 2 - col_off:2 - col_off + NX].reshape(CH, (ZP + 2) * NY * NX)
        back = back + jnp.dot(kernel[:, :, tap].T, window, precision=lax.Precision.HIGHEST)
    scale = 1.0 / math.sqrt(ZP * NY * NX)
    out_field = to_blocks(total.reshape(CH, ZP, NY, NX).astype(jnp.bfloat16))
    in_grad = to_blocks(back.reshape(CH, ZP + 2, NY, NX).astype(jnp.bfloat16))
    weight_grad = jnp.stack(kernel_terms, axis=-1) * scale
    return (out_field, in_grad, weight_grad)
```

```python
import functools
import math

import jax
import jax.numpy as jnp
from jax import lax
from jax.experimental import pallas as pl
from jax.experimental.pallas import tpu as pltpu
from jax.sharding import PartitionSpec as P

ZP = 4


def shifted(value, axis, steps):
    count = lax.axis_size(axis)
    initial, last = (max(0, -steps), min(count, count - steps))
    return lax.ppermute(value, axis, [(source, source + steps) for source in range(initial, last)])


def with_rims(cells, width):
    above = shifted(cells[:, :, -width:], "tile", 1)
    below = shifted(cells[:, :, :width], "tile", -1)
    return jnp.concatenate([above, cells, below], axis=-1)


def tap_copies(tall, width):
    wide = tall.astype(jnp.float32)
    lanes = wide.shape[1]
    col = lax.broadcasted_iota(jnp.int32, wide.shape, 1) % width
    left = jnp.where(col == 0, 0.0, pltpu.roll(wide, 1, 1)).astype(jnp.bfloat16)
    right = jnp.where(col == width - 1, 0.0, pltpu.roll(wide, lanes - 1, 1)).astype(jnp.bfloat16)
    return left, tall, right


def conv_kernel(
    dims, xe_ref, de_ref, wout_ref, win_ref, part_ref, ingrad_ref, wgrad_ref, x9, d9, acc
):
    own, every, height, width = dims
    cells = height * width
    chunk = 2 * width

    def build_x(p, carry):
        copies = tap_copies(xe_ref[p], width)
        for ky in range(3):
            for kx in range(3):
                at = pl.multiple_of(p * (9 * own) + (3 * ky + kx) * own, 16)
                x9[pl.ds(at, own), :] = copies[kx][:, ky * width : ky * width + cells]
        return carry

    lax.fori_loop(0, ZP + 2, build_x, 0)

    def forward(step, carry):
        z = step // (cells // chunk)
        at = pl.multiple_of((step % (cells // chunk)) * chunk, chunk)
        rows = pl.ds(pl.multiple_of(z * (9 * own), 16), 27 * own)
        part_ref[z, :, pl.ds(at, chunk)] = jnp.dot(
            wout_ref[...], x9[rows, pl.ds(at, chunk)], preferred_element_type=jnp.float32
        )
        return carry

    lax.fori_loop(0, ZP * (cells // chunk), forward, 0)

    acc[...] = jnp.zeros_like(acc)

    def backward(p, carry):
        copies = tap_copies(de_ref[p], width)
        for ky in range(3):
            for kx in range(3):
                at = (3 * ky + kx) * every
                d9[at : at + every, :] = copies[kx][:, ky * width : ky * width + cells]

        def part(j, inner):
            at = pl.multiple_of(j * chunk, chunk)
            product = jnp.dot(
                win_ref[...], d9[:, pl.ds(at, chunk)], preferred_element_type=jnp.float32
            )
            for kz in range(3):
                acc[p + kz, :, pl.ds(at, chunk)] += product[kz * own : (kz + 1) * own]
            return inner

        return lax.fori_loop(0, cells // chunk, part, carry)

    lax.fori_loop(0, ZP, backward, 0)
    ingrad_ref[...] = acc[...].astype(jnp.bfloat16)

    wgrad_ref[...] = jnp.zeros_like(wgrad_ref)

    def kernel_terms(step, carry):
        z, kz = step // 3, step % 3
        rows = pl.ds(pl.multiple_of((z + kz) * (9 * own), 16), 9 * own)
        wgrad_ref[kz] += lax.dot_general(
            de_ref[z, :, width : width + cells],
            x9[rows, :],
            (((1,), (1,)), ((), ())),
            preferred_element_type=jnp.float32,
        )
        return carry

    lax.fori_loop(0, ZP * 3, kernel_terms, 0)


def per_device(x_slab, weights, cotangent):
    every, own_real = weights.shape[0], weights.shape[1]
    own = -(-own_real // 16) * 16
    height, width = x_slab.shape[3], x_slab.shape[4]
    cells = height * width
    spare = own - own_real
    flat_x = x_slab[0].transpose(1, 0, 2, 3).reshape(ZP + 2, own_real, cells)
    flat_dy = cotangent[0].transpose(1, 0, 2, 3).reshape(ZP, own_real, cells)
    dy_all = lax.all_gather(flat_dy, "chan", axis=1, tiled=True)
    x_rims = with_rims(flat_x, width)
    d_rims = with_rims(dy_all, width)
    if spare:
        x_rims = jnp.pad(x_rims, ((0, 0), (0, spare), (0, 0)))
        weights = jnp.pad(weights, ((0, 0), (0, spare), (0, 0)))
    w_out = weights.transpose(0, 2, 1).reshape(every, 27 * own)
    w_in = (
        weights.reshape(every, own, 3, 9)[:, :, :, ::-1]
        .transpose(2, 1, 3, 0)
        .reshape(3 * own, 9 * every)
    )
    vmem = pl.BlockSpec(memory_space=pltpu.VMEM)
    part, in_flat, terms = pl.pallas_call(
        functools.partial(conv_kernel, (own, every, height, width)),
        out_shape=(
            jax.ShapeDtypeStruct((ZP, every, cells), jnp.float32),
            jax.ShapeDtypeStruct((ZP + 2, own, cells), jnp.bfloat16),
            jax.ShapeDtypeStruct((3, every, 9 * own), jnp.float32),
        ),
        in_specs=[vmem] * 4,
        out_specs=(vmem,) * 3,
        scratch_shapes=[
            pltpu.VMEM(((ZP + 2) * 9 * own, cells), jnp.bfloat16),
            pltpu.VMEM((9 * every, cells), jnp.bfloat16),
            pltpu.VMEM((ZP + 2, own, cells), jnp.float32),
        ],
        compiler_params=pltpu.CompilerParams(vmem_limit_bytes=48 * 1024 * 1024),
    )(x_rims, d_rims, w_out, w_in)
    total = lax.psum_scatter(part, "chan", scatter_dimension=1, tiled=True)
    out_field = (
        total.astype(jnp.bfloat16)
        .reshape(ZP, own_real, height, width)
        .transpose(1, 0, 2, 3)[None]
    )
    in_grad = (
        in_flat[:, :own_real].reshape(ZP + 2, own_real, height, width).transpose(1, 0, 2, 3)[None]
    )
    scale = 1.0 / math.sqrt(ZP * cells * lax.axis_size("tile"))
    summed = lax.psum(terms, "tile") * scale
    weight_grad = (
        summed.reshape(3, every, 9, own)[..., :own_real]
        .transpose(1, 3, 0, 2)
        .reshape(every, own_real, 27)
    )
    return (out_field, in_grad, weight_grad)


LEVELS = 250.0
BEND = 6.0


def row_codes(value, inverse):
    ratio = jnp.abs(value) * inverse
    bent = ratio * (1.0 + BEND) / (1.0 + BEND * ratio)
    size = jnp.exp2(bent * LEVELS - 0.5 * LEVELS)
    return jnp.where(value < 0.0, -size, size).astype(jnp.bfloat16)


def row_values(codes, largest):
    wide = codes.astype(jnp.float32)
    bent = jnp.log2(jnp.abs(wide)) * (1.0 / LEVELS) + 0.5
    size = bent * largest / ((1.0 + BEND) - BEND * bent)
    return jnp.where(wide < 0.0, -size, size)


def diagonal(count):
    shape = (count, 128)
    return lax.broadcasted_iota(jnp.int32, shape, 0) == lax.broadcasted_iota(jnp.int32, shape, 1)


def fused_kernel(
    dims,
    x_ref,
    dy_ref,
    w_ref,
    out_ref,
    ingrad_ref,
    wgrad_ref,
    xe,
    de,
    x9,
    d9,
    acc,
    wout,
    win,
    both,
    coded,
    incoming,
    scale_out,
    scale_in,
    terms,
    pair_in,
    chip_in,
    final,
    rim_send,
    rim_recv,
    far_send,
    far_recv,
    dy_send,
    dy_recv,
    part_send,
    part_recv,
    scale_send,
    scale_recv,
    pair_send,
    pair_recv,
    chip_send,
    chip_recv,
    last_send,
    last_recv,
):
    own, height, width, tiles, scale = dims
    every = 2 * own
    cells = height * width
    tall = cells + 2 * width
    chunk = 2 * width
    tile, chan = lax.axis_index("tile"), lax.axis_index("chan")
    core, chip, chips = tile % 2, tile // 2, tiles // 2
    half_rows = terms.shape[0] // 2
    piece = half_rows // chips

    def there(t, c):
        return {"tile": t, "chan": c}

    def remote(src, dst, send, recv, to):
        return pltpu.make_async_remote_copy(
            src_ref=src,
            dst_ref=dst,
            send_sem=send,
            recv_sem=recv,
            device_id=to,
            device_id_type=pl.DeviceIdType.MESH,
        )

    barrier = pltpu.get_barrier_semaphore()

    def greet(to):
        pl.semaphore_signal(barrier, inc=1, device_id=to, device_id_type=pl.DeviceIdType.MESH)

    mine = pl.ds(pl.multiple_of(chan * own, 16), own)
    other = pl.ds(pl.multiple_of((1 - chan) * own, 16), own)
    has_above, has_below = tile > 0, tile < tiles - 1
    greet(there(tile, 1 - chan))
    for d in range(1, chips):
        greet(there(((chip + d) % chips) * 2 + core, chan))

    @pl.when(has_above)
    def _():
        greet(there(tile - 1, chan))

    @pl.when(has_below)
    def _():
        greet(there(tile + 1, chan))

    for p in range(ZP):
        de[p, mine, width : width + cells] = dy_ref[:, p].reshape(own, cells)

    expected = chips + jnp.where(has_above, 1, 0) + jnp.where(has_below, 1, 0)
    pl.semaphore_wait(barrier, expected)

    top, bottom = pl.ds(width, width), pl.ds(cells, width)
    rim_top, rim_bottom = pl.ds(0, width), pl.ds(cells + width, width)

    def rim_copies(to, src_lanes, dst_lanes, at):
        return [
            remote(xe.at[:, :, src_lanes], xe.at[:, :, dst_lanes],
                   rim_send.at[at], rim_recv.at[at], there(to, chan)),
            remote(de.at[:, mine, src_lanes], de.at[:, mine, dst_lanes],
                   rim_send.at[at + 1], rim_recv.at[at + 1], there(to, chan)),
        ]

    def downward():
        return rim_copies(tile + 1, bottom, rim_top, 0)

    def upward():
        return rim_copies(tile - 1, top, rim_bottom, 2)

    def far_down(p):
        return remote(de.at[p, other, bottom], de.at[p, other, rim_top],
                      far_send.at[p], far_recv.at[p], there(tile + 1, chan))

    def far_up(p):
        return remote(de.at[p, other, top], de.at[p, other, rim_bottom],
                      far_send.at[ZP + p], far_recv.at[ZP + p], there(tile - 1, chan))

    dy_copies = [
        remote(de.at[p, mine, pl.ds(width, cells)], de.at[p, mine, pl.ds(width, cells)],
               dy_send.at[p], dy_recv.at[p], there(tile, 1 - chan))
        for p in range(ZP)
    ]
    for copy in dy_copies:
        copy.start()
    for p in range(ZP + 2):
        xe[p, :, width : width + cells] = x_ref[:, p].reshape(own, cells)

    @pl.when(has_below)
    def _():
        for copy in downward():
            copy.start()

    @pl.when(has_above)
    def _():
        for copy in upward():
            copy.start()

    dy_waits = [
        remote(de.at[p, other, pl.ds(width, cells)], de.at[p, other, pl.ds(width, cells)],
               dy_send.at[p], dy_recv.at[p], there(tile, 1 - chan))
        for p in range(ZP)
    ]

    @pl.when(tile == 0)
    def _():
        xe[:, :, 0:width] = jnp.zeros((ZP + 2, own, width), jnp.bfloat16)
        de[:, :, 0:width] = jnp.zeros((ZP, every, width), jnp.bfloat16)

    @pl.when(tile == tiles - 1)
    def _():
        xe[:, :, cells + width : tall] = jnp.zeros((ZP + 2, own, width), jnp.bfloat16)
        de[:, :, cells + width : tall] = jnp.zeros((ZP, every, width), jnp.bfloat16)

    wout[...] = w_ref[...].astype(jnp.float32).T.astype(jnp.bfloat16)
    for kz in range(3):
        for r in range(9):
            at = (kz * 9 + 8 - r) * own
            win[kz * own : (kz + 1) * own, r * every : (r + 1) * every] = w_ref[at : at + own, :]
    x9[(ZP + 2) * 9 * own :, :] = jnp.zeros((x9.shape[0] - (ZP + 2) * 9 * own, cells), jnp.bfloat16)
    terms[...] = jnp.zeros_like(terms)
    acc[...] = jnp.zeros_like(acc)

    @pl.when(has_above)
    def _():
        downward()[0].wait_recv()

    @pl.when(has_below)
    def _():
        upward()[0].wait_recv()

    def build_x(p, carry):
        copies = tap_copies(xe[p], width)
        for ky in range(3):
            for kx in range(3):
                at = pl.multiple_of(p * (9 * own) + (3 * ky + kx) * own, 16)
                x9[pl.ds(at, own), :] = copies[kx][:, ky * width : ky * width + cells]
        return carry

    lax.fori_loop(0, ZP + 2, build_x, 0)

    part_copies = [
        remote(coded.at[z], incoming.at[z], part_send.at[z], part_recv.at[z],
               there(tile, 1 - chan))
        for z in range(ZP)
    ]
    scale_copies = [
        remote(scale_out.at[z], scale_in.at[z], scale_send.at[z], scale_recv.at[z],
               there(tile, 1 - chan))
        for z in range(ZP)
    ]
    diag = diagonal(own)
    for z in range(ZP):

        def forward(j, carry):
            at = pl.multiple_of(j * chunk, chunk)
            both[z, :, pl.ds(at, chunk)] = jnp.dot(
                wout[...],
                x9[z * 9 * own : z * 9 * own + 27 * own, pl.ds(at, chunk)],
                preferred_element_type=jnp.float32,
            )
            part = jnp.abs(both[z, other, pl.ds(at, chunk)])
            for k in range(chunk // 128):
                carry = jnp.maximum(carry, part[:, k * 128 : (k + 1) * 128])
            return carry

        top_lanes = lax.fori_loop(0, cells // chunk, forward, jnp.zeros((own, 128), jnp.float32))
        largest = jnp.maximum(jnp.max(top_lanes, axis=1, keepdims=True), 1e-30)
        spread = jnp.sum(jnp.where(diag, largest, 0.0), axis=0, keepdims=True)
        scale_out[z] = jnp.broadcast_to(spread, (8, 128))
        inverse = 1.0 / largest

        def encode(j, carry):
            at = pl.multiple_of(j * chunk, chunk)
            coded[z, :, pl.ds(at, chunk)] = row_codes(both[z, other, pl.ds(at, chunk)], inverse)
            return carry

        lax.fori_loop(0, cells // chunk, encode, 0)
        scale_copies[z].start()
        part_copies[z].start()

    group = 3 * every
    for z in range(ZP):
        dy_waits[z].wait_recv()

        @pl.when(has_below)
        def _():
            far_down(z).start()

        @pl.when(has_above)
        def _():
            far_up(z).start()

        def kernel_terms(kz, carry):
            rows = pl.ds(pl.multiple_of((z + kz) * (9 * own), 16), 512)
            value = lax.dot_general(
                de[z, :, width : width + cells],
                x9[rows, :],
                (((1,), (1,)), ((), ())),
                preferred_element_type=jnp.float32,
            )
            for q in range(4):
                at = pl.multiple_of(q * group + kz * every, 8)
                terms[pl.ds(at, every), :] += value[:, q * 128 : (q + 1) * 128]
            return carry

        lax.fori_loop(0, 3, kernel_terms, 0)

    keep_at = pl.multiple_of(core * half_rows, 8)
    give_at = pl.multiple_of((1 - core) * half_rows, 8)
    neighbour = there(chip * 2 + 1 - core, chan)
    pair_copy = remote(
        terms.at[pl.ds(give_at, half_rows), :], pair_in, pair_send.at[0], pair_recv.at[0], neighbour
    )
    pair_copy.start()

    @pl.when(has_above)
    def _():
        for copy in downward()[1:] + [far_down(p) for p in range(ZP)]:
            copy.wait_recv()

    @pl.when(has_below)
    def _():
        for copy in upward()[1:] + [far_up(p) for p in range(ZP)]:
            copy.wait_recv()

    def backward(p, carry):
        copies = tap_copies(de[p], width)
        for ky in range(3):
            for kx in range(3):
                at = (3 * ky + kx) * every
                d9[at : at + every, :] = copies[kx][:, ky * width : ky * width + cells]

        def part(j, inner):
            at = pl.multiple_of(j * chunk, chunk)
            product = jnp.dot(
                win[...], d9[:, pl.ds(at, chunk)], preferred_element_type=jnp.float32
            )
            for kz in range(3):
                acc[p + kz, :, pl.ds(at, chunk)] += product[kz * own : (kz + 1) * own]
            return inner

        return lax.fori_loop(0, cells // chunk, part, carry)

    lax.fori_loop(0, 1, backward, 0)

    pair_copy.wait_recv()
    terms[pl.ds(keep_at, half_rows), :] += pair_in[...]

    def piece_of(index):
        return pl.ds(pl.multiple_of(keep_at + index * piece, 8), piece)

    chip_copies = []
    for d in range(1, chips):
        to = (chip + d) % chips
        copy = remote(terms.at[piece_of(to), :], chip_in.at[d - 1],
                      chip_send.at[d - 1], chip_recv.at[d - 1], there(to * 2 + core, chan))
        copy.start()
        chip_copies.append(copy)

    lax.fori_loop(1, 3, backward, 0)

    total = terms[piece_of(chip), :]
    for d in range(1, chips):
        chip_copies[d - 1].wait_recv()
        total += chip_in[d - 1]
    final[piece_of(chip), :] = total * scale
    for d in range(1, chips):
        to = (chip + d) % chips
        remote(final.at[piece_of(chip), :], final.at[piece_of(chip), :],
               last_send.at[d - 1], last_recv.at[d - 1], there(to * 2 + core, chan)).start()

    lax.fori_loop(3, ZP, backward, 0)
    for p in range(ZP + 2):
        ingrad_ref[:, p] = acc[p].reshape(own, height, width).astype(jnp.bfloat16)

    for d in range(1, chips):
        source = (chip + chips - d) % chips
        remote(final.at[piece_of(source), :], final.at[piece_of(source), :],
               last_send.at[d - 1], last_recv.at[d - 1], there(source * 2 + core, chan)).wait_recv()
    half = pl.ds(keep_at, half_rows)
    given = pl.ds(give_at, half_rows)
    remote(final.at[half, :], final.at[half, :], pair_send.at[1], pair_recv.at[1], neighbour).start()

    remote(final.at[given, :], final.at[given, :], pair_send.at[1], pair_recv.at[1],
           neighbour).wait_recv()
    for kz in range(3):
        for q in range(4):
            at = q * group + kz * every
            rows = min(128, 9 * own - q * 128)
            to = kz * 9 * own + q * 128
            wgrad_ref[to : to + rows, :] = final[at : at + every, :].T[:rows]

    for z in range(ZP):
        scale_copies[z].wait_recv()
        part_copies[z].wait_recv()
        row = jnp.broadcast_to(scale_in[z, 0:1, :], (own, 128))
        largest = jnp.sum(jnp.where(diag, row, 0.0), axis=1, keepdims=True)

        def decode(j, carry):
            at = pl.multiple_of(j * chunk, chunk)
            lanes = pl.ds(at, chunk)
            both[z, mine, lanes] += row_values(incoming[z, :, lanes], largest)
            return carry

        lax.fori_loop(0, cells // chunk, decode, 0)
        out_ref[:, z] = both[z, mine, :].reshape(own, height, width).astype(jnp.bfloat16)

    @pl.when(has_below)
    def _():
        for copy in downward() + [far_down(p) for p in range(ZP)]:
            copy.wait_send()

    @pl.when(has_above)
    def _():
        for copy in upward() + [far_up(p) for p in range(ZP)]:
            copy.wait_send()

    for copy in dy_copies + part_copies + scale_copies + chip_copies + [pair_copy]:
        copy.wait_send()
    for d in range(1, chips):
        to = (chip + d) % chips
        remote(final.at[piece_of(chip), :], final.at[piece_of(chip), :],
               last_send.at[d - 1], last_recv.at[d - 1], there(to * 2 + core, chan)).wait_send()
    remote(final.at[half, :], final.at[half, :], pair_send.at[1], pair_recv.at[1],
           neighbour).wait_send()


def fused_device(x_slab, weights, cotangent):
    every, own = weights.shape[0], weights.shape[1]
    height, width = x_slab.shape[3], x_slab.shape[4]
    cells = height * width
    tall = cells + 2 * width
    tiles = lax.axis_size("tile")
    chips = tiles // 2
    w_taps = weights.transpose(2, 1, 0).reshape(27 * own, every)
    rows = 4 * 3 * every
    scale = 1.0 / math.sqrt(ZP * cells * tiles)
    vmem = pl.BlockSpec(memory_space=pltpu.VMEM)
    dma = pltpu.SemaphoreType.DMA
    bf16, f32 = jnp.bfloat16, jnp.float32
    out_flat, in_flat, terms = pl.pallas_call(
        functools.partial(fused_kernel, (own, height, width, tiles, scale)),
        out_shape=(
            jax.ShapeDtypeStruct((own, ZP, height, width), bf16),
            jax.ShapeDtypeStruct((own, ZP + 2, height, width), bf16),
            jax.ShapeDtypeStruct((27 * own, every), f32),
        ),
        in_specs=[vmem] * 3,
        out_specs=(vmem,) * 3,
        scratch_shapes=[
            pltpu.VMEM((ZP + 2, own, tall), bf16),
            pltpu.VMEM((ZP, every, tall), bf16),
            pltpu.VMEM(((ZP + 2) * 9 * own + 512 - 9 * own, cells), bf16),
            pltpu.VMEM((9 * every, cells), bf16),
            pltpu.VMEM((ZP + 2, own, cells), f32),
            pltpu.VMEM((every, 27 * own), bf16),
            pltpu.VMEM((3 * own, 9 * every), bf16),
            pltpu.VMEM((ZP, every, cells), f32),
            pltpu.VMEM((ZP, own, cells), bf16),
            pltpu.VMEM((ZP, own, cells), bf16),
            pltpu.VMEM((ZP, 8, 128), f32),
            pltpu.VMEM((ZP, 8, 128), f32),
            pltpu.VMEM((rows, 128), f32),
            pltpu.VMEM((rows // 2, 128), f32),
            pltpu.VMEM((chips - 1, rows // tiles, 128), f32),
            pltpu.VMEM((rows, 128), f32),
            dma((4,)),
            dma((4,)),
            dma((2 * ZP,)),
            dma((2 * ZP,)),
            dma((ZP,)),
            dma((ZP,)),
            dma((ZP,)),
            dma((ZP,)),
            dma((ZP,)),
            dma((ZP,)),
            dma((2,)),
            dma((2,)),
            dma((chips - 1,)),
            dma((chips - 1,)),
            dma((chips - 1,)),
            dma((chips - 1,)),
        ],
        compiler_params=pltpu.CompilerParams(
            vmem_limit_bytes=56 * 1024 * 1024, collective_id=0, has_side_effects=True
        ),
    )(x_slab[0], cotangent[0], w_taps)
    weight_grad = terms.reshape(27, own, every).transpose(2, 1, 0)
    return (out_flat[None], in_flat[None], weight_grad)


def solution(mesh):
    in_specs = (
        P("tile", "chan", None, None, None),
        P(None, "chan", None),
        P("tile", "chan", None, None, None),
    )
    out_specs = (
        P("tile", "chan", None, None, None),
        P("tile", "chan", None, None, None),
        P(None, "chan", None),
    )
    fused = mesh.shape["chan"] == 2 and mesh.shape["tile"] == 16
    return jax.shard_map(
        fused_device if fused else per_device, mesh=mesh, in_specs=in_specs, out_specs=out_specs, check_vma=False
    )
```

```python
import functools
import math

import jax
import jax.numpy as jnp
from jax import lax
from jax.experimental import pallas as pl
from jax.experimental.pallas import tpu as pltpu
from jax.sharding import PartitionSpec as P

ZP = 4


def shifted(value, axis, steps):
    count = lax.axis_size(axis)
    initial, last = (max(0, -steps), min(count, count - steps))
    return lax.ppermute(value, axis, [(source, source + steps) for source in range(initial, last)])


def with_rims(cells, width):
    above = shifted(cells[:, :, -width:], "tile", 1)
    below = shifted(cells[:, :, :width], "tile", -1)
    return jnp.concatenate([above, cells, below], axis=-1)


def tap_copies(tall, width):
    wide = tall.astype(jnp.float32)
    lanes = wide.shape[1]
    col = lax.broadcasted_iota(jnp.int32, wide.shape, 1) % width
    left = jnp.where(col == 0, 0.0, pltpu.roll(wide, 1, 1)).astype(jnp.bfloat16)
    right = jnp.where(col == width - 1, 0.0, pltpu.roll(wide, lanes - 1, 1)).astype(jnp.bfloat16)
    return left, tall, right


def conv_kernel(
    dims, xe_ref, de_ref, wout_ref, win_ref, part_ref, ingrad_ref, wgrad_ref, x9, d9, acc
):
    own, every, height, width = dims
    cells = height * width
    chunk = 2 * width

    def build_x(p, carry):
        copies = tap_copies(xe_ref[p], width)
        for ky in range(3):
            for kx in range(3):
                at = pl.multiple_of(p * (9 * own) + (3 * ky + kx) * own, 16)
                x9[pl.ds(at, own), :] = copies[kx][:, ky * width : ky * width + cells]
        return carry

    lax.fori_loop(0, ZP + 2, build_x, 0)

    def forward(step, carry):
        z = step // (cells // chunk)
        at = pl.multiple_of((step % (cells // chunk)) * chunk, chunk)
        rows = pl.ds(pl.multiple_of(z * (9 * own), 16), 27 * own)
        part_ref[z, :, pl.ds(at, chunk)] = jnp.dot(
            wout_ref[...], x9[rows, pl.ds(at, chunk)], preferred_element_type=jnp.float32
        )
        return carry

    lax.fori_loop(0, ZP * (cells // chunk), forward, 0)

    acc[...] = jnp.zeros_like(acc)

    def backward(p, carry):
        copies = tap_copies(de_ref[p], width)
        for ky in range(3):
            for kx in range(3):
                at = (3 * ky + kx) * every
                d9[at : at + every, :] = copies[kx][:, ky * width : ky * width + cells]

        def part(j, inner):
            at = pl.multiple_of(j * chunk, chunk)
            product = jnp.dot(
                win_ref[...], d9[:, pl.ds(at, chunk)], preferred_element_type=jnp.float32
            )
            for kz in range(3):
                acc[p + kz, :, pl.ds(at, chunk)] += product[kz * own : (kz + 1) * own]
            return inner

        return lax.fori_loop(0, cells // chunk, part, carry)

    lax.fori_loop(0, ZP, backward, 0)
    ingrad_ref[...] = acc[...].astype(jnp.bfloat16)

    wgrad_ref[...] = jnp.zeros_like(wgrad_ref)

    def kernel_terms(step, carry):
        z, kz = step // 3, step % 3
        rows = pl.ds(pl.multiple_of((z + kz) * (9 * own), 16), 9 * own)
        wgrad_ref[kz] += lax.dot_general(
            de_ref[z, :, width : width + cells],
            x9[rows, :],
            (((1,), (1,)), ((), ())),
            preferred_element_type=jnp.float32,
        )
        return carry

    lax.fori_loop(0, ZP * 3, kernel_terms, 0)


def per_device(x_slab, weights, cotangent):
    every, own_real = weights.shape[0], weights.shape[1]
    own = -(-own_real // 16) * 16
    height, width = x_slab.shape[3], x_slab.shape[4]
    cells = height * width
    spare = own - own_real
    flat_x = x_slab[0].transpose(1, 0, 2, 3).reshape(ZP + 2, own_real, cells)
    flat_dy = cotangent[0].transpose(1, 0, 2, 3).reshape(ZP, own_real, cells)
    dy_all = lax.all_gather(flat_dy, "chan", axis=1, tiled=True)
    x_rims = with_rims(flat_x, width)
    d_rims = with_rims(dy_all, width)
    if spare:
        x_rims = jnp.pad(x_rims, ((0, 0), (0, spare), (0, 0)))
        weights = jnp.pad(weights, ((0, 0), (0, spare), (0, 0)))
    w_out = weights.transpose(0, 2, 1).reshape(every, 27 * own)
    w_in = (
        weights.reshape(every, own, 3, 9)[:, :, :, ::-1]
        .transpose(2, 1, 3, 0)
        .reshape(3 * own, 9 * every)
    )
    vmem = pl.BlockSpec(memory_space=pltpu.VMEM)
    part, in_flat, terms = pl.pallas_call(
        functools.partial(conv_kernel, (own, every, height, width)),
        out_shape=(
            jax.ShapeDtypeStruct((ZP, every, cells), jnp.float32),
            jax.ShapeDtypeStruct((ZP + 2, own, cells), jnp.bfloat16),
            jax.ShapeDtypeStruct((3, every, 9 * own), jnp.float32),
        ),
        in_specs=[vmem] * 4,
        out_specs=(vmem,) * 3,
        scratch_shapes=[
            pltpu.VMEM(((ZP + 2) * 9 * own, cells), jnp.bfloat16),
            pltpu.VMEM((9 * every, cells), jnp.bfloat16),
            pltpu.VMEM((ZP + 2, own, cells), jnp.float32),
        ],
        compiler_params=pltpu.CompilerParams(vmem_limit_bytes=48 * 1024 * 1024),
    )(x_rims, d_rims, w_out, w_in)
    total = lax.psum_scatter(part, "chan", scatter_dimension=1, tiled=True)
    out_field = (
        total.astype(jnp.bfloat16)
        .reshape(ZP, own_real, height, width)
        .transpose(1, 0, 2, 3)[None]
    )
    in_grad = (
        in_flat[:, :own_real].reshape(ZP + 2, own_real, height, width).transpose(1, 0, 2, 3)[None]
    )
    scale = 1.0 / math.sqrt(ZP * cells * lax.axis_size("tile"))
    summed = lax.psum(terms, "tile") * scale
    weight_grad = (
        summed.reshape(3, every, 9, own)[..., :own_real]
        .transpose(1, 3, 0, 2)
        .reshape(every, own_real, 27)
    )
    return (out_field, in_grad, weight_grad)


LEVELS = 250.0
BEND = 3.0


def row_codes(value, inverse):
    ratio = jnp.abs(value) * inverse
    bent = ratio * (1.0 + BEND) / (1.0 + BEND * ratio)
    size = jnp.exp2(bent * LEVELS - 0.5 * LEVELS)
    return jnp.where(value < 0.0, -size, size).astype(jnp.bfloat16)


def row_values(codes, largest):
    wide = codes.astype(jnp.float32)
    bent = jnp.log2(jnp.abs(wide)) * (1.0 / LEVELS) + 0.5
    size = bent * largest / ((1.0 + BEND) - BEND * bent)
    return jnp.where(wide < 0.0, -size, size)


def diagonal(count):
    shape = (count, 128)
    return lax.broadcasted_iota(jnp.int32, shape, 0) == lax.broadcasted_iota(jnp.int32, shape, 1)


def fused_kernel(
    dims,
    x_ref,
    dy_ref,
    w_ref,
    out_ref,
    ingrad_ref,
    wgrad_ref,
    xe,
    de,
    x9,
    d9,
    acc,
    wout,
    win,
    both,
    coded,
    incoming,
    scale_out,
    scale_in,
    sums,
    terms,
    pair_in,
    chip_in,
    final,
    rim_send,
    rim_recv,
    far_send,
    far_recv,
    dy_send,
    dy_recv,
    part_send,
    part_recv,
    scale_send,
    scale_recv,
    pair_send,
    pair_recv,
    chip_send,
    chip_recv,
    last_send,
    last_recv,
    back_send,
    back_recv,
):
    own, height, width, tiles, scale = dims
    every = 2 * own
    taps = 9 * own
    cells = height * width
    tall = cells + 2 * width
    tile, chan = lax.axis_index("tile"), lax.axis_index("chan")
    core, chip, chips = tile % 2, tile // 2, tiles // 2
    half_rows = terms.shape[1] // 2
    piece = half_rows // chips
    f32, bf16 = jnp.float32, jnp.bfloat16

    def there(t, c):
        return {"tile": t, "chan": c}

    def remote(src, dst, send, recv, to):
        return pltpu.make_async_remote_copy(
            src_ref=src,
            dst_ref=dst,
            send_sem=send,
            recv_sem=recv,
            device_id=to,
            device_id_type=pl.DeviceIdType.MESH,
        )

    barrier = pltpu.get_barrier_semaphore()

    def greet(to):
        pl.semaphore_signal(barrier, inc=1, device_id=to, device_id_type=pl.DeviceIdType.MESH)

    has_above, has_below = tile > 0, tile < tiles - 1
    greet(there(tile, 1 - chan))
    for d in range(1, chips):
        greet(there(((chip + d) % chips) * 2 + core, chan))

    @pl.when(has_above)
    def _():
        greet(there(tile - 1, chan))

    @pl.when(has_below)
    def _():
        greet(there(tile + 1, chan))

    middle = pl.ds(width, cells)
    for p in range(ZP):
        de[0, p, :, width : width + cells] = dy_ref[:, p].reshape(own, cells)
    for p in range(ZP + 2):
        xe[p, :, width : width + cells] = x_ref[:, p].reshape(own, cells)

    @pl.when(tile == 0)
    def _():
        xe[:, :, 0:width] = jnp.zeros((ZP + 2, own, width), bf16)
        de[:, :, :, 0:width] = jnp.zeros((2, ZP, own, width), bf16)

    @pl.when(tile == tiles - 1)
    def _():
        xe[:, :, cells + width : tall] = jnp.zeros((ZP + 2, own, width), bf16)
        de[:, :, :, cells + width : tall] = jnp.zeros((2, ZP, own, width), bf16)

    whole = w_ref[...].astype(f32)
    swapped = jnp.concatenate([whole[:, own:], whole[:, :own]], axis=1)
    ordered = jnp.where(chan == 0, whole, swapped)
    for kz in range(3):
        wout[(2 - kz) * every : (3 - kz) * every, :] = (
            ordered[kz * taps : (kz + 1) * taps].T.astype(bf16)
        )
    ordered = ordered.astype(bf16)
    for kz in range(3):
        for r in range(9):
            at = (kz * 9 + 8 - r) * own
            for h in range(2):
                win[h, kz * own : (kz + 1) * own, r * own : (r + 1) * own] = (
                    ordered[at : at + own, h * own : (h + 1) * own]
                )

    expected = chips + jnp.where(has_above, 1, 0) + jnp.where(has_below, 1, 0)
    pl.semaphore_wait(barrier, expected)

    top, bottom = pl.ds(width, width), pl.ds(cells, width)
    rim_top, rim_bottom = pl.ds(0, width), pl.ds(cells + width, width)
    partner = there(tile, 1 - chan)

    dy_copies = [
        remote(de.at[0, p, :, middle], de.at[1, p, :, middle], dy_send.at[p], dy_recv.at[p], partner)
        for p in range(ZP)
    ]
    for copy in dy_copies:
        copy.start()

    def rim_copies(to, src_lanes, dst_lanes, at):
        return [
            remote(xe.at[:, :, src_lanes], xe.at[:, :, dst_lanes],
                   rim_send.at[at], rim_recv.at[at], there(to, chan)),
            remote(de.at[0, :, :, src_lanes], de.at[0, :, :, dst_lanes],
                   rim_send.at[at + 1], rim_recv.at[at + 1], there(to, chan)),
        ]

    def downward():
        return rim_copies(tile + 1, bottom, rim_top, 0)

    def upward():
        return rim_copies(tile - 1, top, rim_bottom, 2)

    def far_down():
        return remote(de.at[1, :, :, bottom], de.at[1, :, :, rim_top],
                      far_send.at[0], far_recv.at[0], there(tile + 1, chan))

    def far_up():
        return remote(de.at[1, :, :, top], de.at[1, :, :, rim_bottom],
                      far_send.at[1], far_recv.at[1], there(tile - 1, chan))

    @pl.when(has_below)
    def _():
        for copy in downward():
            copy.start()

    @pl.when(has_above)
    def _():
        for copy in upward():
            copy.start()

    @pl.when(has_above)
    def _():
        for copy in downward():
            copy.wait_recv()

    @pl.when(has_below)
    def _():
        for copy in upward():
            copy.wait_recv()

    part_copies = [
        remote(coded.at[z], incoming.at[z], part_send.at[z], part_recv.at[z], partner)
        for z in range(ZP)
    ]
    scale_copies = [
        remote(scale_out.at[z], scale_in.at[z], scale_send.at[z], scale_recv.at[z], partner)
        for z in range(ZP)
    ]
    diag = diagonal(own)
    chunk = 2 * width

    def encode(z):
        lanes = jnp.zeros((own, 128), f32)
        for at in range(0, cells, 128):
            lanes = jnp.maximum(lanes, jnp.abs(both[z, own:every, at : at + 128]))
        largest = jnp.maximum(jnp.max(lanes, axis=1, keepdims=True), 1e-30)
        spread = jnp.sum(jnp.where(diag, largest, 0.0), axis=0, keepdims=True)
        scale_out[z] = jnp.broadcast_to(spread, (8, 128))
        inverse = 1.0 / largest
        for at in range(0, cells, chunk):
            coded[z, :, at : at + chunk] = row_codes(both[z, own:every, at : at + chunk], inverse)

    def build(value, target, at):
        copies = tap_copies(value, width)
        for ky in range(3):
            for kx in range(3):
                row = at + (3 * ky + kx) * own
                target[row : row + own, :] = copies[kx][:, ky * width : ky * width + cells]

    def planes_of(p):
        return max(0, p - 2), min(ZP - 1, p)

    for p in range(ZP + 2):
        build(xe[p], x9, p * taps)
        first, last = planes_of(p)
        low = (first - p + 2) * every
        product = jnp.dot(
            wout[low : low + (last - first + 1) * every, :],
            x9[p * taps : (p + 1) * taps, :],
            preferred_element_type=f32,
        )
        for z in range(first, last + 1):
            block = product[(z - first) * every : (z - first + 1) * every]
            if z == p:
                both[z] = block
            else:
                both[z] += block
        if p >= 2:
            encode(p - 2)

    def kernel_terms(h):
        for p in range(ZP + 2):
            first, last = planes_of(p)
            count = last - first + 1
            value = lax.dot_general(
                de[h, first : last + 1, :, width : width + cells].reshape(count * own, cells),
                x9[p * taps : (p + 1) * taps, :],
                (((1,), (1,)), ((), ())),
                preferred_element_type=f32,
            )
            low = (first - p + 2) * own
            if p == 0:
                sums[h] = jnp.zeros_like(sums[h])
            sums[h, low : low + count * own, 0:taps] += value
        for q in range(3):
            terms[h, q * 3 * own : (q + 1) * 3 * own, :] = sums[h, :, q * 128 : (q + 1) * 128]
        rest = sums[h, :, 384:512]
        lane = lax.broadcasted_iota(jnp.int32, (own, 128), 1)
        packed = jnp.where(lane < own, rest[0:own], pltpu.roll(rest[own : 2 * own], own, 1))
        terms[h, 9 * own : 10 * own, :] = packed
        lane = lax.broadcasted_iota(jnp.int32, (own // 2, 128), 1)
        lower, upper = rest[2 * own : 2 * own + own // 2], rest[2 * own + own // 2 :]
        packed = jnp.where(lane < own, lower, pltpu.roll(upper, own, 1))
        terms[h, 10 * own : 10 * own + own // 2, :] = packed
        left = terms.shape[1] - (10 * own + own // 2)
        terms[h, 10 * own + own // 2 :, :] = jnp.zeros((left, 128), f32)

    keep_at = pl.multiple_of(core * half_rows, 8)
    give_at = pl.multiple_of((1 - core) * half_rows, 8)
    keep, give = pl.ds(keep_at, half_rows), pl.ds(give_at, half_rows)
    neighbour = there(chip * 2 + 1 - core, chan)

    def piece_of(index):
        return pl.ds(pl.multiple_of(keep_at + index * piece, 8), piece)

    pair_copies = [
        remote(terms.at[h, give, :], pair_in.at[h], pair_send.at[h], pair_recv.at[h], neighbour)
        for h in range(2)
    ]

    def chip_copy(h, d):
        to = (chip + d) % chips
        return remote(terms.at[h, piece_of(to), :], chip_in.at[h, d - 1],
                      chip_send.at[h, d - 1], chip_recv.at[h, d - 1], there(to * 2 + core, chan))

    def last_copy(h, d):
        to = (chip + d) % chips
        return remote(final.at[h, piece_of(chip), :], final.at[h, piece_of(chip), :],
                      last_send.at[h, d - 1], last_recv.at[h, d - 1], there(to * 2 + core, chan))

    def last_arrival(h, d):
        source = (chip + chips - d) % chips
        return remote(final.at[h, piece_of(source), :], final.at[h, piece_of(source), :],
                      last_send.at[h, d - 1], last_recv.at[h, d - 1],
                      there(source * 2 + core, chan))

    def back_copy(h):
        return remote(final.at[h, keep, :], final.at[h, keep, :],
                      back_send.at[h], back_recv.at[h], neighbour)

    def back_arrival(h):
        return remote(final.at[h, give, :], final.at[h, give, :],
                      back_send.at[h], back_recv.at[h], neighbour)

    def to_chips(h):
        pair_copies[h].wait_recv()
        terms[h, keep, :] += pair_in[h]
        for d in range(1, chips):
            chip_copy(h, d).start()

    def from_chips(h):
        total = terms[h, piece_of(chip), :]
        for d in range(1, chips):
            chip_copy(h, d).wait_recv()
            total += chip_in[h, d - 1]
        final[h, piece_of(chip), :] = total * scale
        for d in range(1, chips):
            last_copy(h, d).start()

    def to_pair(h):
        for d in range(1, chips):
            last_arrival(h, d).wait_recv()
        back_copy(h).start()

    def backward(h, p):
        build(de[h, p], d9.at[p % 2], 0)
        product = jnp.dot(win[h], d9[p % 2], preferred_element_type=f32)
        for kz in range(3):
            block = product[kz * own : (kz + 1) * own]
            if h == 0 and (p == 0 or kz == 2):
                acc[p + kz] = block
            else:
                acc[p + kz] += block

    kernel_terms(0)
    pair_copies[0].start()
    for p in range(2):
        backward(0, p)
    to_chips(0)
    for p in range(2, ZP):
        backward(0, p)

    for z in range(ZP):
        dy_copies[z].wait_send()
        scale_copies[z].start()
        part_copies[z].start()
    for z in range(ZP):
        dy_copies[z].wait_recv()

    @pl.when(has_below)
    def _():
        far_down().start()

    @pl.when(has_above)
    def _():
        far_up().start()

    kernel_terms(1)
    pair_copies[1].start()
    from_chips(0)

    @pl.when(has_above)
    def _():
        far_down().wait_recv()

    @pl.when(has_below)
    def _():
        far_up().wait_recv()

    def finish(s):
        ingrad_ref[:, s] = acc[s].reshape(own, height, width).astype(bf16)

    backward(1, 0)
    finish(0)
    to_chips(1)
    for p in range(1, ZP):
        backward(1, p)
        finish(p)
    finish(ZP)
    finish(ZP + 1)
    to_pair(0)

    def decode(z):
        scale_copies[z].wait_recv()
        part_copies[z].wait_recv()
        row = jnp.broadcast_to(scale_in[z, 0:1, :], (own, 128))
        largest = jnp.sum(jnp.where(diag, row, 0.0), axis=1, keepdims=True)
        for at in range(0, cells, chunk):
            total = both[z, 0:own, at : at + chunk] + row_values(
                incoming[z, :, at : at + chunk], largest
            )
            lines = slice(at // width, (at + chunk) // width)
            out_ref[:, z, lines] = total.reshape(own, chunk // width, width).astype(bf16)

    from_chips(1)
    decode(0)
    decode(1)
    to_pair(1)
    decode(2)

    halves = []
    for h in range(2):
        back_arrival(h).wait_recv()
        rows = [final[h, q * 3 * own : (q + 1) * 3 * own, :] for q in range(3)]
        one = final[h, 9 * own : 10 * own, :]
        two = final[h, 10 * own : 10 * own + own // 2, :]
        rest = jnp.concatenate(
            [one, pltpu.roll(one, 128 - own, 1), two, pltpu.roll(two, 128 - own, 1)], axis=0
        )
        halves.append(jnp.concatenate(rows + [rest], axis=1))
    for kz in range(3):
        low = (2 - kz) * own
        mine, other = (halves[h][low : low + own].T[:taps] for h in range(2))
        wgrad_ref[kz * taps : (kz + 1) * taps, :] = jnp.where(
            chan == 0,
            jnp.concatenate([mine, other], axis=1),
            jnp.concatenate([other, mine], axis=1),
        )
    decode(ZP - 1)

    @pl.when(has_below)
    def _():
        for copy in downward() + [far_down()]:
            copy.wait_send()

    @pl.when(has_above)
    def _():
        for copy in upward() + [far_up()]:
            copy.wait_send()

    for copy in part_copies + scale_copies + pair_copies:
        copy.wait_send()
    for h in range(2):
        for d in range(1, chips):
            chip_copy(h, d).wait_send()
            last_copy(h, d).wait_send()
        back_copy(h).wait_send()


def fused_device(x_slab, weights, cotangent):
    every, own = weights.shape[0], weights.shape[1]
    height, width = x_slab.shape[3], x_slab.shape[4]
    cells = height * width
    tall = cells + 2 * width
    tiles = lax.axis_size("tile")
    chips = tiles // 2
    w_taps = weights.transpose(2, 1, 0).reshape(27 * own, every)
    taps = 9 * own
    rows = -(-(10 * own + own // 2) // (16 * chips)) * (16 * chips)
    scale = 1.0 / math.sqrt(ZP * cells * tiles)
    vmem = pl.BlockSpec(memory_space=pltpu.VMEM)
    dma = pltpu.SemaphoreType.DMA
    bf16, f32 = jnp.bfloat16, jnp.float32
    out_flat, in_flat, terms = pl.pallas_call(
        functools.partial(fused_kernel, (own, height, width, tiles, scale)),
        out_shape=(
            jax.ShapeDtypeStruct((own, ZP, height, width), bf16),
            jax.ShapeDtypeStruct((own, ZP + 2, height, width), bf16),
            jax.ShapeDtypeStruct((27 * own, every), f32),
        ),
        in_specs=[vmem] * 3,
        out_specs=(vmem,) * 3,
        scratch_shapes=[
            pltpu.VMEM((ZP + 2, own, tall), bf16),
            pltpu.VMEM((2, ZP, own, tall), bf16),
            pltpu.VMEM(((ZP + 2) * taps, cells), bf16),
            pltpu.VMEM((2, taps, cells), bf16),
            pltpu.VMEM((ZP + 2, own, cells), f32),
            pltpu.VMEM((3 * every, taps), bf16),
            pltpu.VMEM((2, 3 * own, taps), bf16),
            pltpu.VMEM((ZP, every, cells), f32),
            pltpu.VMEM((ZP, own, cells), bf16),
            pltpu.VMEM((ZP, own, cells), bf16),
            pltpu.VMEM((ZP, 8, 128), f32),
            pltpu.VMEM((ZP, 8, 128), f32),
            pltpu.VMEM((2, 3 * own, 512), f32),
            pltpu.VMEM((2, rows, 128), f32),
            pltpu.VMEM((2, rows // 2, 128), f32),
            pltpu.VMEM((2, chips - 1, rows // tiles, 128), f32),
            pltpu.VMEM((2, rows, 128), f32),
            dma((4,)),
            dma((4,)),
            dma((2,)),
            dma((2,)),
            dma((ZP,)),
            dma((ZP,)),
            dma((ZP,)),
            dma((ZP,)),
            dma((ZP,)),
            dma((ZP,)),
            dma((2,)),
            dma((2,)),
            dma((2, chips - 1)),
            dma((2, chips - 1)),
            dma((2, chips - 1)),
            dma((2, chips - 1)),
            dma((2,)),
            dma((2,)),
        ],
        compiler_params=pltpu.CompilerParams(
            vmem_limit_bytes=60 * 1024 * 1024, collective_id=0, has_side_effects=True
        ),
    )(x_slab[0], cotangent[0], w_taps)
    weight_grad = terms.reshape(27, own, every).transpose(2, 1, 0)
    return (out_flat[None], in_flat[None], weight_grad)


def solution(mesh):
    in_specs = (
        P("tile", "chan", None, None, None),
        P(None, "chan", None),
        P("tile", "chan", None, None, None),
    )
    out_specs = (
        P("tile", "chan", None, None, None),
        P("tile", "chan", None, None, None),
        P(None, "chan", None),
    )
    fused = mesh.shape["chan"] == 2 and mesh.shape["tile"] == 16
    return jax.shard_map(
        fused_device if fused else per_device, mesh=mesh, in_specs=in_specs, out_specs=out_specs, check_vma=False
    )
```

```python
import functools
import math

import jax
import jax.numpy as jnp
from jax import lax
from jax.experimental import pallas as pl
from jax.experimental.pallas import tpu as pltpu
from jax.sharding import PartitionSpec as P

ZP = 4


def shifted(value, axis, steps):
    count = lax.axis_size(axis)
    initial, last = (max(0, -steps), min(count, count - steps))
    return lax.ppermute(value, axis, [(source, source + steps) for source in range(initial, last)])


def with_rims(cells, width):
    above = shifted(cells[:, :, -width:], "tile", 1)
    below = shifted(cells[:, :, :width], "tile", -1)
    return jnp.concatenate([above, cells, below], axis=-1)


def tap_copies(tall, width):
    wide = tall.astype(jnp.float32)
    lanes = wide.shape[1]
    col = lax.broadcasted_iota(jnp.int32, wide.shape, 1) % width
    left = jnp.where(col == 0, 0.0, pltpu.roll(wide, 1, 1)).astype(jnp.bfloat16)
    right = jnp.where(col == width - 1, 0.0, pltpu.roll(wide, lanes - 1, 1)).astype(jnp.bfloat16)
    return left, tall, right


def conv_kernel(
    dims, xe_ref, de_ref, wout_ref, win_ref, part_ref, ingrad_ref, wgrad_ref, x9, d9, acc
):
    own, every, height, width = dims
    cells = height * width
    chunk = 2 * width

    def build_x(p, carry):
        copies = tap_copies(xe_ref[p], width)
        for ky in range(3):
            for kx in range(3):
                at = pl.multiple_of(p * (9 * own) + (3 * ky + kx) * own, 16)
                x9[pl.ds(at, own), :] = copies[kx][:, ky * width : ky * width + cells]
        return carry

    lax.fori_loop(0, ZP + 2, build_x, 0)

    def forward(step, carry):
        z = step // (cells // chunk)
        at = pl.multiple_of((step % (cells // chunk)) * chunk, chunk)
        rows = pl.ds(pl.multiple_of(z * (9 * own), 16), 27 * own)
        part_ref[z, :, pl.ds(at, chunk)] = jnp.dot(
            wout_ref[...], x9[rows, pl.ds(at, chunk)], preferred_element_type=jnp.float32
        )
        return carry

    lax.fori_loop(0, ZP * (cells // chunk), forward, 0)

    acc[...] = jnp.zeros_like(acc)

    def backward(p, carry):
        copies = tap_copies(de_ref[p], width)
        for ky in range(3):
            for kx in range(3):
                at = (3 * ky + kx) * every
                d9[at : at + every, :] = copies[kx][:, ky * width : ky * width + cells]

        def part(j, inner):
            at = pl.multiple_of(j * chunk, chunk)
            product = jnp.dot(
                win_ref[...], d9[:, pl.ds(at, chunk)], preferred_element_type=jnp.float32
            )
            for kz in range(3):
                acc[p + kz, :, pl.ds(at, chunk)] += product[kz * own : (kz + 1) * own]
            return inner

        return lax.fori_loop(0, cells // chunk, part, carry)

    lax.fori_loop(0, ZP, backward, 0)
    ingrad_ref[...] = acc[...].astype(jnp.bfloat16)

    wgrad_ref[...] = jnp.zeros_like(wgrad_ref)

    def kernel_terms(step, carry):
        z, kz = step // 3, step % 3
        rows = pl.ds(pl.multiple_of((z + kz) * (9 * own), 16), 9 * own)
        wgrad_ref[kz] += lax.dot_general(
            de_ref[z, :, width : width + cells],
            x9[rows, :],
            (((1,), (1,)), ((), ())),
            preferred_element_type=jnp.float32,
        )
        return carry

    lax.fori_loop(0, ZP * 3, kernel_terms, 0)


def per_device(x_slab, weights, cotangent):
    every, own_real = weights.shape[0], weights.shape[1]
    own = -(-own_real // 16) * 16
    height, width = x_slab.shape[3], x_slab.shape[4]
    cells = height * width
    spare = own - own_real
    flat_x = x_slab[0].transpose(1, 0, 2, 3).reshape(ZP + 2, own_real, cells)
    flat_dy = cotangent[0].transpose(1, 0, 2, 3).reshape(ZP, own_real, cells)
    dy_all = lax.all_gather(flat_dy, "chan", axis=1, tiled=True)
    x_rims = with_rims(flat_x, width)
    d_rims = with_rims(dy_all, width)
    if spare:
        x_rims = jnp.pad(x_rims, ((0, 0), (0, spare), (0, 0)))
        weights = jnp.pad(weights, ((0, 0), (0, spare), (0, 0)))
    w_out = weights.transpose(0, 2, 1).reshape(every, 27 * own)
    w_in = (
        weights.reshape(every, own, 3, 9)[:, :, :, ::-1]
        .transpose(2, 1, 3, 0)
        .reshape(3 * own, 9 * every)
    )
    vmem = pl.BlockSpec(memory_space=pltpu.VMEM)
    part, in_flat, terms = pl.pallas_call(
        functools.partial(conv_kernel, (own, every, height, width)),
        out_shape=(
            jax.ShapeDtypeStruct((ZP, every, cells), jnp.float32),
            jax.ShapeDtypeStruct((ZP + 2, own, cells), jnp.bfloat16),
            jax.ShapeDtypeStruct((3, every, 9 * own), jnp.float32),
        ),
        in_specs=[vmem] * 4,
        out_specs=(vmem,) * 3,
        scratch_shapes=[
            pltpu.VMEM(((ZP + 2) * 9 * own, cells), jnp.bfloat16),
            pltpu.VMEM((9 * every, cells), jnp.bfloat16),
            pltpu.VMEM((ZP + 2, own, cells), jnp.float32),
        ],
        compiler_params=pltpu.CompilerParams(vmem_limit_bytes=48 * 1024 * 1024),
    )(x_rims, d_rims, w_out, w_in)
    total = lax.psum_scatter(part, "chan", scatter_dimension=1, tiled=True)
    out_field = (
        total.astype(jnp.bfloat16)
        .reshape(ZP, own_real, height, width)
        .transpose(1, 0, 2, 3)[None]
    )
    in_grad = (
        in_flat[:, :own_real].reshape(ZP + 2, own_real, height, width).transpose(1, 0, 2, 3)[None]
    )
    scale = 1.0 / math.sqrt(ZP * cells * lax.axis_size("tile"))
    summed = lax.psum(terms, "tile") * scale
    weight_grad = (
        summed.reshape(3, every, 9, own)[..., :own_real]
        .transpose(1, 3, 0, 2)
        .reshape(every, own_real, 27)
    )
    return (out_field, in_grad, weight_grad)


LEVELS = 250.0
BEND = 3.0


def row_codes(value, inverse):
    ratio = jnp.abs(value) * inverse
    bent = ratio * (1.0 + BEND) / (1.0 + BEND * ratio)
    size = jnp.exp2(bent * LEVELS - 0.5 * LEVELS)
    return jnp.where(value < 0.0, -size, size).astype(jnp.bfloat16)


def row_values(codes, largest):
    wide = codes.astype(jnp.float32)
    bent = jnp.log2(jnp.abs(wide)) * (1.0 / LEVELS) + 0.5
    size = bent * largest / ((1.0 + BEND) - BEND * bent)
    return jnp.where(wide < 0.0, -size, size)


def diagonal(count):
    shape = (count, 128)
    return lax.broadcasted_iota(jnp.int32, shape, 0) == lax.broadcasted_iota(jnp.int32, shape, 1)


def fused_kernel(
    dims,
    x_hbm,
    dy_hbm,
    w_hbm,
    out_ref,
    ingrad_ref,
    wgrad_ref,
    x_ref,
    dy_ref,
    w_ref,
    load_sem,
    xe,
    de,
    x9,
    d9,
    acc,
    wout,
    win,
    both,
    coded,
    incoming,
    scale_out,
    scale_in,
    sums,
    terms,
    pair_in,
    chip_in,
    final,
    rim_send,
    rim_recv,
    far_send,
    far_recv,
    dy_send,
    dy_recv,
    part_send,
    part_recv,
    scale_send,
    scale_recv,
    pair_send,
    pair_recv,
    chip_send,
    chip_recv,
    last_send,
    last_recv,
    back_send,
    back_recv,
):
    own, height, width, tiles, scale = dims
    every = 2 * own
    taps = 9 * own
    cells = height * width
    tall = cells + 2 * width
    tile, chan = lax.axis_index("tile"), lax.axis_index("chan")
    core, chip, chips = tile % 2, tile // 2, tiles // 2
    half_rows = terms.shape[1] // 2
    piece = half_rows // chips
    f32, bf16 = jnp.float32, jnp.bfloat16

    def there(t, c):
        return {"tile": t, "chan": c}

    def remote(src, dst, send, recv, to):
        return pltpu.make_async_remote_copy(
            src_ref=src,
            dst_ref=dst,
            send_sem=send,
            recv_sem=recv,
            device_id=to,
            device_id_type=pl.DeviceIdType.MESH,
        )

    barrier = pltpu.get_barrier_semaphore()

    def greet(to):
        pl.semaphore_signal(barrier, inc=1, device_id=to, device_id_type=pl.DeviceIdType.MESH)

    has_above, has_below = tile > 0, tile < tiles - 1
    greet(there(tile, 1 - chan))
    for d in range(1, chips):
        greet(there(((chip + d) % chips) * 2 + core, chan))

    @pl.when(has_above)
    def _():
        greet(there(tile - 1, chan))

    @pl.when(has_below)
    def _():
        greet(there(tile + 1, chan))

    loads = [
        pltpu.make_async_copy(source, target, load_sem.at[k])
        for k, (source, target) in enumerate(((dy_hbm, dy_ref), (x_hbm, x_ref), (w_hbm, w_ref)))
    ]
    for load in loads:
        load.start()
    middle = pl.ds(width, cells)
    loads[0].wait()
    for p in range(ZP):
        de[0, p, :, width : width + cells] = dy_ref[:, p].reshape(own, cells)
    loads[1].wait()
    for p in range(ZP + 2):
        xe[p, :, width : width + cells] = x_ref[:, p].reshape(own, cells)

    @pl.when(tile == 0)
    def _():
        xe[:, :, 0:width] = jnp.zeros((ZP + 2, own, width), bf16)
        de[:, :, :, 0:width] = jnp.zeros((2, ZP, own, width), bf16)

    @pl.when(tile == tiles - 1)
    def _():
        xe[:, :, cells + width : tall] = jnp.zeros((ZP + 2, own, width), bf16)
        de[:, :, :, cells + width : tall] = jnp.zeros((2, ZP, own, width), bf16)

    loads[2].wait()
    whole = w_ref[...].astype(f32)
    swapped = jnp.concatenate([whole[:, own:], whole[:, :own]], axis=1)
    ordered = jnp.where(chan == 0, whole, swapped)
    for kz in range(3):
        wout[(2 - kz) * every : (3 - kz) * every, :] = (
            ordered[kz * taps : (kz + 1) * taps].T.astype(bf16)
        )
    ordered = ordered.astype(bf16)
    for kz in range(3):
        for r in range(9):
            at = (kz * 9 + 8 - r) * own
            for h in range(2):
                win[h, kz * own : (kz + 1) * own, r * own : (r + 1) * own] = (
                    ordered[at : at + own, h * own : (h + 1) * own]
                )

    expected = chips + jnp.where(has_above, 1, 0) + jnp.where(has_below, 1, 0)
    pl.semaphore_wait(barrier, expected)

    top, bottom = pl.ds(width, width), pl.ds(cells, width)
    rim_top, rim_bottom = pl.ds(0, width), pl.ds(cells + width, width)
    partner = there(tile, 1 - chan)

    dy_copies = [
        remote(de.at[0, p, :, middle], de.at[1, p, :, middle], dy_send.at[p], dy_recv.at[p], partner)
        for p in range(ZP)
    ]
    for copy in dy_copies:
        copy.start()

    def rim_copies(to, src_lanes, dst_lanes, at):
        return [
            remote(xe.at[:, :, src_lanes], xe.at[:, :, dst_lanes],
                   rim_send.at[at], rim_recv.at[at], there(to, chan)),
            remote(de.at[0, :, :, src_lanes], de.at[0, :, :, dst_lanes],
                   rim_send.at[at + 1], rim_recv.at[at + 1], there(to, chan)),
        ]

    def downward():
        return rim_copies(tile + 1, bottom, rim_top, 0)

    def upward():
        return rim_copies(tile - 1, top, rim_bottom, 2)

    def far_down():
        return remote(de.at[1, :, :, bottom], de.at[1, :, :, rim_top],
                      far_send.at[0], far_recv.at[0], there(tile + 1, chan))

    def far_up():
        return remote(de.at[1, :, :, top], de.at[1, :, :, rim_bottom],
                      far_send.at[1], far_recv.at[1], there(tile - 1, chan))

    @pl.when(has_below)
    def _():
        for copy in downward():
            copy.start()

    @pl.when(has_above)
    def _():
        for copy in upward():
            copy.start()

    @pl.when(has_above)
    def _():
        for copy in downward():
            copy.wait_recv()

    @pl.when(has_below)
    def _():
        for copy in upward():
            copy.wait_recv()

    part_copies = [
        remote(coded.at[z], incoming.at[z], part_send.at[z], part_recv.at[z], partner)
        for z in range(ZP)
    ]
    scale_copies = [
        remote(scale_out.at[z], scale_in.at[z], scale_send.at[z], scale_recv.at[z], partner)
        for z in range(ZP)
    ]
    diag = diagonal(own)
    chunk = 2 * width

    def encode(z):
        lanes = jnp.zeros((own, 128), f32)
        for at in range(0, cells, 128):
            lanes = jnp.maximum(lanes, jnp.abs(both[z, own:every, at : at + 128]))
        largest = jnp.maximum(jnp.max(lanes, axis=1, keepdims=True), 1e-30)
        spread = jnp.sum(jnp.where(diag, largest, 0.0), axis=0, keepdims=True)
        scale_out[z] = jnp.broadcast_to(spread, (8, 128))
        inverse = 1.0 / largest
        for at in range(0, cells, chunk):
            coded[z, :, at : at + chunk] = row_codes(both[z, own:every, at : at + chunk], inverse)

    def build(value, target, at):
        copies = tap_copies(value, width)
        for ky in range(3):
            for kx in range(3):
                row = at + (3 * ky + kx) * own
                target[row : row + own, :] = copies[kx][:, ky * width : ky * width + cells]

    def planes_of(p):
        return max(0, p - 2), min(ZP - 1, p)

    for p in range(ZP + 2):
        build(xe[p], x9, p * taps)
        first, last = planes_of(p)
        low = (first - p + 2) * every
        product = jnp.dot(
            wout[low : low + (last - first + 1) * every, :],
            x9[p * taps : (p + 1) * taps, :],
            preferred_element_type=f32,
        )
        for z in range(first, last + 1):
            block = product[(z - first) * every : (z - first + 1) * every]
            if z == p:
                both[z] = block
            else:
                both[z] += block
        if p >= 2:
            encode(p - 2)

    def kernel_terms(h):
        for p in range(ZP + 2):
            first, last = planes_of(p)
            count = last - first + 1
            value = lax.dot_general(
                de[h, first : last + 1, :, width : width + cells].reshape(count * own, cells),
                x9[p * taps : (p + 1) * taps, :],
                (((1,), (1,)), ((), ())),
                preferred_element_type=f32,
            )
            low = (first - p + 2) * own
            if p == 0:
                sums[h] = jnp.zeros_like(sums[h])
            sums[h, low : low + count * own, 0:taps] += value
        for q in range(3):
            terms[h, q * 3 * own : (q + 1) * 3 * own, :] = sums[h, :, q * 128 : (q + 1) * 128]
        rest = sums[h, :, 384:512]
        lane = lax.broadcasted_iota(jnp.int32, (own, 128), 1)
        packed = jnp.where(lane < own, rest[0:own], pltpu.roll(rest[own : 2 * own], own, 1))
        terms[h, 9 * own : 10 * own, :] = packed
        lane = lax.broadcasted_iota(jnp.int32, (own // 2, 128), 1)
        lower, upper = rest[2 * own : 2 * own + own // 2], rest[2 * own + own // 2 :]
        packed = jnp.where(lane < own, lower, pltpu.roll(upper, own, 1))
        terms[h, 10 * own : 10 * own + own // 2, :] = packed
        left = terms.shape[1] - (10 * own + own // 2)
        terms[h, 10 * own + own // 2 :, :] = jnp.zeros((left, 128), f32)

    keep_at = pl.multiple_of(core * half_rows, 8)
    give_at = pl.multiple_of((1 - core) * half_rows, 8)
    keep, give = pl.ds(keep_at, half_rows), pl.ds(give_at, half_rows)
    neighbour = there(chip * 2 + 1 - core, chan)

    def piece_of(index):
        return pl.ds(pl.multiple_of(keep_at + index * piece, 8), piece)

    pair_copies = [
        remote(terms.at[h, give, :], pair_in.at[h], pair_send.at[h], pair_recv.at[h], neighbour)
        for h in range(2)
    ]

    def chip_copy(h, d):
        to = (chip + d) % chips
        return remote(terms.at[h, piece_of(to), :], chip_in.at[h, d - 1],
                      chip_send.at[h, d - 1], chip_recv.at[h, d - 1], there(to * 2 + core, chan))

    def last_copy(h, d):
        to = (chip + d) % chips
        return remote(final.at[h, piece_of(chip), :], final.at[h, piece_of(chip), :],
                      last_send.at[h, d - 1], last_recv.at[h, d - 1], there(to * 2 + core, chan))

    def last_arrival(h, d):
        source = (chip + chips - d) % chips
        return remote(final.at[h, piece_of(source), :], final.at[h, piece_of(source), :],
                      last_send.at[h, d - 1], last_recv.at[h, d - 1],
                      there(source * 2 + core, chan))

    def back_copy(h):
        return remote(final.at[h, keep, :], final.at[h, keep, :],
                      back_send.at[h], back_recv.at[h], neighbour)

    def back_arrival(h):
        return remote(final.at[h, give, :], final.at[h, give, :],
                      back_send.at[h], back_recv.at[h], neighbour)

    def to_chips(h):
        pair_copies[h].wait_recv()
        terms[h, keep, :] += pair_in[h]
        for d in range(1, chips):
            chip_copy(h, d).start()

    def from_chips(h):
        total = terms[h, piece_of(chip), :]
        for d in range(1, chips):
            chip_copy(h, d).wait_recv()
            total += chip_in[h, d - 1]
        final[h, piece_of(chip), :] = total * scale
        for d in range(1, chips):
            last_copy(h, d).start()

    def to_pair(h):
        for d in range(1, chips):
            last_arrival(h, d).wait_recv()
        back_copy(h).start()

    def backward(h, p):
        build(de[h, p], d9.at[p % 2], 0)
        product = jnp.dot(win[h], d9[p % 2], preferred_element_type=f32)
        for kz in range(3):
            block = product[kz * own : (kz + 1) * own]
            if h == 0 and (p == 0 or kz == 2):
                acc[p + kz] = block
            else:
                acc[p + kz] += block

    kernel_terms(0)
    pair_copies[0].start()
    for p in range(2):
        backward(0, p)
    to_chips(0)
    for p in range(2, ZP):
        backward(0, p)

    for z in range(ZP):
        dy_copies[z].wait_send()
        scale_copies[z].start()
        part_copies[z].start()
    for z in range(ZP):
        dy_copies[z].wait_recv()

    @pl.when(has_below)
    def _():
        far_down().start()

    @pl.when(has_above)
    def _():
        far_up().start()

    kernel_terms(1)
    pair_copies[1].start()
    from_chips(0)

    @pl.when(has_above)
    def _():
        far_down().wait_recv()

    @pl.when(has_below)
    def _():
        far_up().wait_recv()

    def finish(s):
        ingrad_ref[:, s] = acc[s].reshape(own, height, width).astype(bf16)

    backward(1, 0)
    finish(0)
    to_chips(1)
    for p in range(1, ZP):
        backward(1, p)
        finish(p)
    finish(ZP)
    finish(ZP + 1)
    to_pair(0)

    def decode(z):
        scale_copies[z].wait_recv()
        part_copies[z].wait_recv()
        row = jnp.broadcast_to(scale_in[z, 0:1, :], (own, 128))
        largest = jnp.sum(jnp.where(diag, row, 0.0), axis=1, keepdims=True)
        for at in range(0, cells, chunk):
            total = both[z, 0:own, at : at + chunk] + row_values(
                incoming[z, :, at : at + chunk], largest
            )
            lines = slice(at // width, (at + chunk) // width)
            out_ref[:, z, lines] = total.reshape(own, chunk // width, width).astype(bf16)

    from_chips(1)
    decode(0)
    decode(1)
    to_pair(1)
    decode(2)

    halves = []
    for h in range(2):
        back_arrival(h).wait_recv()
        rows = [final[h, q * 3 * own : (q + 1) * 3 * own, :] for q in range(3)]
        one = final[h, 9 * own : 10 * own, :]
        two = final[h, 10 * own : 10 * own + own // 2, :]
        rest = jnp.concatenate(
            [one, pltpu.roll(one, 128 - own, 1), two, pltpu.roll(two, 128 - own, 1)], axis=0
        )
        halves.append(jnp.concatenate(rows + [rest], axis=1))
    for kz in range(3):
        low = (2 - kz) * own
        mine, other = (halves[h][low : low + own].T[:taps] for h in range(2))
        wgrad_ref[kz * taps : (kz + 1) * taps, :] = jnp.where(
            chan == 0,
            jnp.concatenate([mine, other], axis=1),
            jnp.concatenate([other, mine], axis=1),
        )
    decode(ZP - 1)

    @pl.when(has_below)
    def _():
        for copy in downward() + [far_down()]:
            copy.wait_send()

    @pl.when(has_above)
    def _():
        for copy in upward() + [far_up()]:
            copy.wait_send()

    for copy in part_copies + scale_copies + pair_copies:
        copy.wait_send()
    for h in range(2):
        for d in range(1, chips):
            chip_copy(h, d).wait_send()
            last_copy(h, d).wait_send()
        back_copy(h).wait_send()


def write_kernel(a_ref, b_ref, c_ref, a_out, b_out, c_out, sems):
    copies = [
        pltpu.make_async_copy(source, target, sems.at[k])
        for k, (source, target) in enumerate(((a_ref, a_out), (b_ref, b_out), (c_ref, c_out)))
    ]
    for copy in copies:
        copy.start()
    for copy in copies:
        copy.wait()


def fused_device(x_slab, weights, cotangent):
    every, own = weights.shape[0], weights.shape[1]
    height, width = x_slab.shape[3], x_slab.shape[4]
    cells = height * width
    tall = cells + 2 * width
    tiles = lax.axis_size("tile")
    chips = tiles // 2
    w_taps = weights.transpose(2, 1, 0).reshape(27 * own, every)
    taps = 9 * own
    rows = -(-(10 * own + own // 2) // (16 * chips)) * (16 * chips)
    scale = 1.0 / math.sqrt(ZP * cells * tiles)
    vmem = pl.BlockSpec(memory_space=pltpu.VMEM)
    dma = pltpu.SemaphoreType.DMA
    bf16, f32 = jnp.bfloat16, jnp.float32
    hbm = pl.BlockSpec(memory_space=pl.ANY)
    shapes = (
        ((own, ZP, height, width), bf16),
        ((own, ZP + 2, height, width), bf16),
        ((27 * own, every), f32),
    )
    held = pl.pallas_call(
        functools.partial(fused_kernel, (own, height, width, tiles, scale)),
        out_shape=tuple(pltpu.VMEM(*shape) for shape in shapes),
        in_specs=[hbm] * 3,
        out_specs=(vmem,) * 3,
        scratch_shapes=[
            pltpu.VMEM((own, ZP + 2, height, width), bf16),
            pltpu.VMEM((own, ZP, height, width), bf16),
            pltpu.VMEM((27 * own, every), bf16),
            dma((3,)),
            pltpu.VMEM((ZP + 2, own, tall), bf16),
            pltpu.VMEM((2, ZP, own, tall), bf16),
            pltpu.VMEM(((ZP + 2) * taps, cells), bf16),
            pltpu.VMEM((2, taps, cells), bf16),
            pltpu.VMEM((ZP + 2, own, cells), f32),
            pltpu.VMEM((3 * every, taps), bf16),
            pltpu.VMEM((2, 3 * own, taps), bf16),
            pltpu.VMEM((ZP, every, cells), f32),
            pltpu.VMEM((ZP, own, cells), bf16),
            pltpu.VMEM((ZP, own, cells), bf16),
            pltpu.VMEM((ZP, 8, 128), f32),
            pltpu.VMEM((ZP, 8, 128), f32),
            pltpu.VMEM((2, 3 * own, 512), f32),
            pltpu.VMEM((2, rows, 128), f32),
            pltpu.VMEM((2, rows // 2, 128), f32),
            pltpu.VMEM((2, chips - 1, rows // tiles, 128), f32),
            pltpu.VMEM((2, rows, 128), f32),
            dma((4,)),
            dma((4,)),
            dma((2,)),
            dma((2,)),
            dma((ZP,)),
            dma((ZP,)),
            dma((ZP,)),
            dma((ZP,)),
            dma((ZP,)),
            dma((ZP,)),
            dma((2,)),
            dma((2,)),
            dma((2, chips - 1)),
            dma((2, chips - 1)),
            dma((2, chips - 1)),
            dma((2, chips - 1)),
            dma((2,)),
            dma((2,)),
        ],
        compiler_params=pltpu.CompilerParams(
            vmem_limit_bytes=58 * 1024 * 1024, collective_id=0, has_side_effects=True
        ),
    )(x_slab[0], cotangent[0], w_taps)
    out_flat, in_flat, terms = pl.pallas_call(
        write_kernel,
        out_shape=tuple(jax.ShapeDtypeStruct(*shape) for shape in shapes),
        in_specs=[hbm] * 3,
        out_specs=(hbm,) * 3,
        scratch_shapes=[dma((3,))],
        compiler_params=pltpu.CompilerParams(vmem_limit_bytes=1024 * 1024),
    )(*(pltpu.with_memory_space_constraint(value, pltpu.VMEM) for value in held))
    weight_grad = terms.reshape(27, own, every).transpose(2, 1, 0)
    return (out_flat[None], in_flat[None], weight_grad)


def solution(mesh):
    in_specs = (
        P("tile", "chan", None, None, None),
        P(None, "chan", None),
        P("tile", "chan", None, None, None),
    )
    out_specs = (
        P("tile", "chan", None, None, None),
        P("tile", "chan", None, None, None),
        P(None, "chan", None),
    )
    fused = mesh.shape["chan"] == 2 and mesh.shape["tile"] == 16
    return jax.shard_map(
        fused_device if fused else per_device, mesh=mesh, in_specs=in_specs, out_specs=out_specs, check_vma=False
    )
```

```python
import functools
import math

import jax
import jax.numpy as jnp
from jax import lax
from jax.experimental import pallas as pl
from jax.experimental.pallas import tpu as pltpu
from jax.sharding import PartitionSpec as P

ZP = 4


def shifted(value, axis, steps):
    count = lax.axis_size(axis)
    initial, last = (max(0, -steps), min(count, count - steps))
    return lax.ppermute(value, axis, [(source, source + steps) for source in range(initial, last)])


def with_rims(cells, width):
    above = shifted(cells[:, :, -width:], "tile", 1)
    below = shifted(cells[:, :, :width], "tile", -1)
    return jnp.concatenate([above, cells, below], axis=-1)


def tap_copies(tall, width):
    wide = tall.astype(jnp.float32)
    lanes = wide.shape[1]
    col = lax.broadcasted_iota(jnp.int32, wide.shape, 1) % width
    left = jnp.where(col == 0, 0.0, pltpu.roll(wide, 1, 1)).astype(jnp.bfloat16)
    right = jnp.where(col == width - 1, 0.0, pltpu.roll(wide, lanes - 1, 1)).astype(jnp.bfloat16)
    return left, tall, right


def conv_kernel(
    dims, xe_ref, de_ref, wout_ref, win_ref, part_ref, ingrad_ref, wgrad_ref, x9, d9, acc
):
    own, every, height, width = dims
    cells = height * width
    chunk = 2 * width

    def build_x(p, carry):
        copies = tap_copies(xe_ref[p], width)
        for ky in range(3):
            for kx in range(3):
                at = pl.multiple_of(p * (9 * own) + (3 * ky + kx) * own, 16)
                x9[pl.ds(at, own), :] = copies[kx][:, ky * width : ky * width + cells]
        return carry

    lax.fori_loop(0, ZP + 2, build_x, 0)

    def forward(step, carry):
        z = step // (cells // chunk)
        at = pl.multiple_of((step % (cells // chunk)) * chunk, chunk)
        rows = pl.ds(pl.multiple_of(z * (9 * own), 16), 27 * own)
        part_ref[z, :, pl.ds(at, chunk)] = jnp.dot(
            wout_ref[...], x9[rows, pl.ds(at, chunk)], preferred_element_type=jnp.float32
        )
        return carry

    lax.fori_loop(0, ZP * (cells // chunk), forward, 0)

    acc[...] = jnp.zeros_like(acc)

    def backward(p, carry):
        copies = tap_copies(de_ref[p], width)
        for ky in range(3):
            for kx in range(3):
                at = (3 * ky + kx) * every
                d9[at : at + every, :] = copies[kx][:, ky * width : ky * width + cells]

        def part(j, inner):
            at = pl.multiple_of(j * chunk, chunk)
            product = jnp.dot(
                win_ref[...], d9[:, pl.ds(at, chunk)], preferred_element_type=jnp.float32
            )
            for kz in range(3):
                acc[p + kz, :, pl.ds(at, chunk)] += product[kz * own : (kz + 1) * own]
            return inner

        return lax.fori_loop(0, cells // chunk, part, carry)

    lax.fori_loop(0, ZP, backward, 0)
    ingrad_ref[...] = acc[...].astype(jnp.bfloat16)

    wgrad_ref[...] = jnp.zeros_like(wgrad_ref)

    def kernel_terms(step, carry):
        z, kz = step // 3, step % 3
        rows = pl.ds(pl.multiple_of((z + kz) * (9 * own), 16), 9 * own)
        wgrad_ref[kz] += lax.dot_general(
            de_ref[z, :, width : width + cells],
            x9[rows, :],
            (((1,), (1,)), ((), ())),
            preferred_element_type=jnp.float32,
        )
        return carry

    lax.fori_loop(0, ZP * 3, kernel_terms, 0)


def per_device(x_slab, weights, cotangent):
    every, own_real = weights.shape[0], weights.shape[1]
    own = -(-own_real // 16) * 16
    height, width = x_slab.shape[3], x_slab.shape[4]
    cells = height * width
    spare = own - own_real
    flat_x = x_slab[0].transpose(1, 0, 2, 3).reshape(ZP + 2, own_real, cells)
    flat_dy = cotangent[0].transpose(1, 0, 2, 3).reshape(ZP, own_real, cells)
    dy_all = lax.all_gather(flat_dy, "chan", axis=1, tiled=True)
    x_rims = with_rims(flat_x, width)
    d_rims = with_rims(dy_all, width)
    if spare:
        x_rims = jnp.pad(x_rims, ((0, 0), (0, spare), (0, 0)))
        weights = jnp.pad(weights, ((0, 0), (0, spare), (0, 0)))
    w_out = weights.transpose(0, 2, 1).reshape(every, 27 * own)
    w_in = (
        weights.reshape(every, own, 3, 9)[:, :, :, ::-1]
        .transpose(2, 1, 3, 0)
        .reshape(3 * own, 9 * every)
    )
    vmem = pl.BlockSpec(memory_space=pltpu.VMEM)
    part, in_flat, terms = pl.pallas_call(
        functools.partial(conv_kernel, (own, every, height, width)),
        out_shape=(
            jax.ShapeDtypeStruct((ZP, every, cells), jnp.float32),
            jax.ShapeDtypeStruct((ZP + 2, own, cells), jnp.bfloat16),
            jax.ShapeDtypeStruct((3, every, 9 * own), jnp.float32),
        ),
        in_specs=[vmem] * 4,
        out_specs=(vmem,) * 3,
        scratch_shapes=[
            pltpu.VMEM(((ZP + 2) * 9 * own, cells), jnp.bfloat16),
            pltpu.VMEM((9 * every, cells), jnp.bfloat16),
            pltpu.VMEM((ZP + 2, own, cells), jnp.float32),
        ],
        compiler_params=pltpu.CompilerParams(vmem_limit_bytes=48 * 1024 * 1024),
    )(x_rims, d_rims, w_out, w_in)
    total = lax.psum_scatter(part, "chan", scatter_dimension=1, tiled=True)
    out_field = (
        total.astype(jnp.bfloat16)
        .reshape(ZP, own_real, height, width)
        .transpose(1, 0, 2, 3)[None]
    )
    in_grad = (
        in_flat[:, :own_real].reshape(ZP + 2, own_real, height, width).transpose(1, 0, 2, 3)[None]
    )
    scale = 1.0 / math.sqrt(ZP * cells * lax.axis_size("tile"))
    summed = lax.psum(terms, "tile") * scale
    weight_grad = (
        summed.reshape(3, every, 9, own)[..., :own_real]
        .transpose(1, 3, 0, 2)
        .reshape(every, own_real, 27)
    )
    return (out_field, in_grad, weight_grad)


LEVELS = 250.0
BEND = 3.0


def row_codes(value, inverse):
    ratio = jnp.abs(value) * inverse
    bent = ratio * (1.0 + BEND) / (1.0 + BEND * ratio)
    size = jnp.exp2(bent * LEVELS - 0.5 * LEVELS)
    return jnp.where(value < 0.0, -size, size).astype(jnp.bfloat16)


def row_values(codes, largest):
    wide = codes.astype(jnp.float32)
    bent = jnp.log2(jnp.abs(wide)) * (1.0 / LEVELS) + 0.5
    size = bent * largest / ((1.0 + BEND) - BEND * bent)
    return jnp.where(wide < 0.0, -size, size)


def diagonal(count):
    shape = (count, 128)
    return lax.broadcasted_iota(jnp.int32, shape, 0) == lax.broadcasted_iota(jnp.int32, shape, 1)


def fused_kernel(
    dims,
    x_hbm,
    dy_hbm,
    w_hbm,
    out_ref,
    ingrad_ref,
    wgrad_ref,
    x_ref,
    dy_ref,
    w_ref,
    load_sem,
    entered,
    xe,
    de,
    x9,
    d9,
    acc,
    wout,
    win,
    both,
    coded,
    incoming,
    scale_out,
    scale_in,
    sums,
    terms,
    pair_in,
    chip_in,
    final,
    rim_send,
    rim_recv,
    far_send,
    far_recv,
    dy_send,
    dy_recv,
    part_send,
    part_recv,
    scale_send,
    scale_recv,
    pair_send,
    pair_recv,
    chip_send,
    chip_recv,
    last_send,
    last_recv,
    back_send,
    back_recv,
):
    own, height, width, tiles, scale = dims
    every = 2 * own
    taps = 9 * own
    cells = height * width
    tall = cells + 2 * width
    tile, chan = lax.axis_index("tile"), lax.axis_index("chan")
    core, chip, chips = tile % 2, tile // 2, tiles // 2
    half_rows = terms.shape[1] // 2
    piece = half_rows // chips
    f32, bf16 = jnp.float32, jnp.bfloat16

    def there(t, c):
        return {"tile": t, "chan": c}

    def remote(src, dst, send, recv, to):
        return pltpu.make_async_remote_copy(
            src_ref=src,
            dst_ref=dst,
            send_sem=send,
            recv_sem=recv,
            device_id=to,
            device_id_type=pl.DeviceIdType.MESH,
        )

    barrier = pltpu.get_barrier_semaphore()

    def greet(to):
        pl.semaphore_signal(barrier, inc=1, device_id=to, device_id_type=pl.DeviceIdType.MESH)

    has_above, has_below = tile > 0, tile < tiles - 1
    greet(there(tile, 1 - chan))

    @pl.when(has_above)
    def _():
        greet(there(tile - 1, chan))

    @pl.when(has_below)
    def _():
        greet(there(tile + 1, chan))

    loads = [
        pltpu.make_async_copy(source, target, load_sem.at[k])
        for k, (source, target) in enumerate(
            [(dy_hbm.at[:, p], dy_ref.at[:, p]) for p in range(ZP)]
            + [(x_hbm, x_ref), (w_hbm, w_ref)]
        )
    ]
    for load in loads:
        load.start()
    middle = pl.ds(width, cells)
    partner = there(tile, 1 - chan)
    dy_copies = [
        remote(de.at[0, p, :, middle], de.at[1, p, :, middle], dy_send.at[p], dy_recv.at[p], partner)
        for p in range(ZP)
    ]
    for p in range(ZP):
        loads[p].wait()
        de[0, p, :, width : width + cells] = dy_ref[:, p].reshape(own, cells)
        if p == 0:
            expected = 1 + jnp.where(has_above, 1, 0) + jnp.where(has_below, 1, 0)
            pl.semaphore_wait(barrier, expected)
        dy_copies[p].start()
    loads[ZP].wait()
    for p in range(ZP + 2):
        xe[p, :, width : width + cells] = x_ref[:, p].reshape(own, cells)

    @pl.when(tile == 0)
    def _():
        xe[:, :, 0:width] = jnp.zeros((ZP + 2, own, width), bf16)
        de[:, :, :, 0:width] = jnp.zeros((2, ZP, own, width), bf16)

    @pl.when(tile == tiles - 1)
    def _():
        xe[:, :, cells + width : tall] = jnp.zeros((ZP + 2, own, width), bf16)
        de[:, :, :, cells + width : tall] = jnp.zeros((2, ZP, own, width), bf16)

    top, bottom = pl.ds(width, width), pl.ds(cells, width)
    rim_top, rim_bottom = pl.ds(0, width), pl.ds(cells + width, width)

    def rim_copies(to, src_lanes, dst_lanes, at):
        return [
            remote(xe.at[:, :, src_lanes], xe.at[:, :, dst_lanes],
                   rim_send.at[at], rim_recv.at[at], there(to, chan)),
            remote(de.at[0, :, :, src_lanes], de.at[0, :, :, dst_lanes],
                   rim_send.at[at + 1], rim_recv.at[at + 1], there(to, chan)),
        ]

    def downward():
        return rim_copies(tile + 1, bottom, rim_top, 0)

    def upward():
        return rim_copies(tile - 1, top, rim_bottom, 2)

    def far_down():
        return remote(de.at[1, :, :, bottom], de.at[1, :, :, rim_top],
                      far_send.at[0], far_recv.at[0], there(tile + 1, chan))

    def far_up():
        return remote(de.at[1, :, :, top], de.at[1, :, :, rim_bottom],
                      far_send.at[1], far_recv.at[1], there(tile - 1, chan))

    @pl.when(has_below)
    def _():
        for copy in downward():
            copy.start()

    @pl.when(has_above)
    def _():
        for copy in upward():
            copy.start()

    def tell(k):
        step = 2**k

        @pl.when(tile >= step)
        def _():
            pl.semaphore_signal(entered.at[k], inc=1, device_id=there(tile - step, chan),
                                device_id_type=pl.DeviceIdType.MESH)

        @pl.when(tile < tiles - step)
        def _():
            pl.semaphore_signal(entered.at[k], inc=1, device_id=there(tile + step, chan),
                                device_id_type=pl.DeviceIdType.MESH)

    def hear(k):
        step = 2**k
        pl.semaphore_wait(
            entered.at[k], jnp.where(tile >= step, 1, 0) + jnp.where(tile < tiles - step, 1, 0)
        )

    rounds = (tiles - 1).bit_length()
    tell(0)

    loads[ZP + 1].wait()
    whole = w_ref[...].astype(f32)
    swapped = jnp.concatenate([whole[:, own:], whole[:, :own]], axis=1)
    ordered = jnp.where(chan == 0, whole, swapped)
    for kz in range(3):
        wout[(2 - kz) * every : (3 - kz) * every, :] = (
            ordered[kz * taps : (kz + 1) * taps].T.astype(bf16)
        )
    ordered = ordered.astype(bf16)
    for kz in range(3):
        for r in range(9):
            at = (kz * 9 + 8 - r) * own
            for h in range(2):
                win[h, kz * own : (kz + 1) * own, r * own : (r + 1) * own] = (
                    ordered[at : at + own, h * own : (h + 1) * own]
                )


    @pl.when(has_above)
    def _():
        for copy in downward():
            copy.wait_recv()

    @pl.when(has_below)
    def _():
        for copy in upward():
            copy.wait_recv()

    part_copies = [
        remote(coded.at[z], incoming.at[z], part_send.at[z], part_recv.at[z], partner)
        for z in range(ZP)
    ]
    scale_copies = [
        remote(scale_out.at[z], scale_in.at[z], scale_send.at[z], scale_recv.at[z], partner)
        for z in range(ZP)
    ]
    diag = diagonal(own)
    chunk = 2 * width

    def encode(z):
        lanes = jnp.zeros((own, 128), f32)
        for at in range(0, cells, 128):
            lanes = jnp.maximum(lanes, jnp.abs(both[z, own:every, at : at + 128]))
        largest = jnp.maximum(jnp.max(lanes, axis=1, keepdims=True), 1e-30)
        spread = jnp.sum(jnp.where(diag, largest, 0.0), axis=0, keepdims=True)
        scale_out[z] = jnp.broadcast_to(spread, (8, 128))
        inverse = 1.0 / largest
        for at in range(0, cells, chunk):
            coded[z, :, at : at + chunk] = row_codes(both[z, own:every, at : at + chunk], inverse)

    def build(value, target, at):
        copies = tap_copies(value, width)
        for ky in range(3):
            for kx in range(3):
                row = at + (3 * ky + kx) * own
                target[row : row + own, :] = copies[kx][:, ky * width : ky * width + cells]

    def planes_of(p):
        return max(0, p - 2), min(ZP - 1, p)

    for p in range(ZP + 2):
        build(xe[p], x9, p * taps)
        first, last = planes_of(p)
        low = (first - p + 2) * every
        product = jnp.dot(
            wout[low : low + (last - first + 1) * every, :],
            x9[p * taps : (p + 1) * taps, :],
            preferred_element_type=f32,
        )
        for z in range(first, last + 1):
            block = product[(z - first) * every : (z - first + 1) * every]
            if z == p:
                both[z] = block
            else:
                both[z] += block
        if p >= 2:
            encode(p - 2)
        if p in (1, 4) and p // 3 + 1 < rounds:
            hear(p // 3)
            tell(p // 3 + 1)

    def kernel_terms(h):
        for p in range(ZP + 2):
            first, last = planes_of(p)
            count = last - first + 1
            if h == 1 and p == 0:
                for copy in dy_copies:
                    copy.wait_recv()
            if h == 1 and p == 0:

                @pl.when(has_below)
                def _():
                    far_down().start()

                @pl.when(has_above)
                def _():
                    far_up().start()

            value = lax.dot_general(
                de[h, first : last + 1, :, width : width + cells].reshape(count * own, cells),
                x9[p * taps : (p + 1) * taps, :],
                (((1,), (1,)), ((), ())),
                preferred_element_type=f32,
            )
            low = (first - p + 2) * own
            if p == 0:
                sums[h] = jnp.zeros_like(sums[h])
            sums[h, low : low + count * own, 0:taps] += value
        for q in range(3):
            terms[h, q * 3 * own : (q + 1) * 3 * own, :] = sums[h, :, q * 128 : (q + 1) * 128]
        rest = sums[h, :, 384:512]
        lane = lax.broadcasted_iota(jnp.int32, (own, 128), 1)
        packed = jnp.where(lane < own, rest[0:own], pltpu.roll(rest[own : 2 * own], own, 1))
        terms[h, 9 * own : 10 * own, :] = packed
        lane = lax.broadcasted_iota(jnp.int32, (own // 2, 128), 1)
        lower, upper = rest[2 * own : 2 * own + own // 2], rest[2 * own + own // 2 :]
        packed = jnp.where(lane < own, lower, pltpu.roll(upper, own, 1))
        terms[h, 10 * own : 10 * own + own // 2, :] = packed
        left = terms.shape[1] - (10 * own + own // 2)
        terms[h, 10 * own + own // 2 :, :] = jnp.zeros((left, 128), f32)

    keep_at = pl.multiple_of(core * half_rows, 8)
    give_at = pl.multiple_of((1 - core) * half_rows, 8)
    keep, give = pl.ds(keep_at, half_rows), pl.ds(give_at, half_rows)
    neighbour = there(chip * 2 + 1 - core, chan)

    def piece_of(index):
        return pl.ds(pl.multiple_of(keep_at + index * piece, 8), piece)

    pair_copies = [
        remote(terms.at[h, give, :], pair_in.at[h], pair_send.at[h], pair_recv.at[h], neighbour)
        for h in range(2)
    ]

    def chip_copy(h, d):
        to = (chip + d) % chips
        return remote(terms.at[h, piece_of(to), :], chip_in.at[h, d - 1],
                      chip_send.at[h, d - 1], chip_recv.at[h, d - 1], there(to * 2 + core, chan))

    def last_copy(h, d):
        to = (chip + d) % chips
        return remote(final.at[h, piece_of(chip), :], final.at[h, piece_of(chip), :],
                      last_send.at[h, d - 1], last_recv.at[h, d - 1], there(to * 2 + core, chan))

    def last_arrival(h, d):
        source = (chip + chips - d) % chips
        return remote(final.at[h, piece_of(source), :], final.at[h, piece_of(source), :],
                      last_send.at[h, d - 1], last_recv.at[h, d - 1],
                      there(source * 2 + core, chan))

    def back_copy(h):
        return remote(final.at[h, keep, :], final.at[h, keep, :],
                      back_send.at[h], back_recv.at[h], neighbour)

    def back_arrival(h):
        return remote(final.at[h, give, :], final.at[h, give, :],
                      back_send.at[h], back_recv.at[h], neighbour)

    def to_chips(h):
        pair_copies[h].wait_recv()
        terms[h, keep, :] += pair_in[h]
        for d in range(1, chips):
            chip_copy(h, d).start()

    def from_chips(h):
        total = terms[h, piece_of(chip), :]
        for d in range(1, chips):
            chip_copy(h, d).wait_recv()
            total += chip_in[h, d - 1]
        final[h, piece_of(chip), :] = total * scale
        for d in range(1, chips):
            last_copy(h, d).start()

    def to_pair(h):
        for d in range(1, chips):
            last_arrival(h, d).wait_recv()
        back_copy(h).start()

    def backward(h, p):
        build(de[h, p], d9.at[p % 2], 0)
        product = jnp.dot(win[h], d9[p % 2], preferred_element_type=f32)
        for kz in range(3):
            block = product[kz * own : (kz + 1) * own]
            if h == 0 and (p == 0 or kz == 2):
                acc[p + kz] = block
            else:
                acc[p + kz] += block

    kernel_terms(0)
    pair_copies[0].start()
    for k in range(2, rounds):
        hear(k)
        if k + 1 < rounds:
            tell(k + 1)
        backward(0, k - 2)
    for p in range(max(0, rounds - 2), ZP):
        backward(0, p)
    to_chips(0)

    for z in range(ZP):
        dy_copies[z].wait_send()
        scale_copies[z].start()
        part_copies[z].start()
    kernel_terms(1)
    pair_copies[1].start()
    from_chips(0)

    @pl.when(has_above)
    def _():
        far_down().wait_recv()

    @pl.when(has_below)
    def _():
        far_up().wait_recv()

    def finish(s):
        ingrad_ref[:, s] = acc[s].reshape(own, height, width).astype(bf16)

    backward(1, 0)
    finish(0)
    to_chips(1)
    for p in range(1, ZP):
        backward(1, p)
        finish(p)
    finish(ZP)
    finish(ZP + 1)
    to_pair(0)

    def decode(z):
        scale_copies[z].wait_recv()
        part_copies[z].wait_recv()
        row = jnp.broadcast_to(scale_in[z, 0:1, :], (own, 128))
        largest = jnp.sum(jnp.where(diag, row, 0.0), axis=1, keepdims=True)
        for at in range(0, cells, chunk):
            total = both[z, 0:own, at : at + chunk] + row_values(
                incoming[z, :, at : at + chunk], largest
            )
            lines = slice(at // width, (at + chunk) // width)
            out_ref[:, z, lines] = total.reshape(own, chunk // width, width).astype(bf16)

    from_chips(1)
    decode(0)
    decode(1)
    to_pair(1)
    decode(2)

    halves = []
    for h in range(2):
        back_arrival(h).wait_recv()
        rows = [final[h, q * 3 * own : (q + 1) * 3 * own, :] for q in range(3)]
        one = final[h, 9 * own : 10 * own, :]
        two = final[h, 10 * own : 10 * own + own // 2, :]
        rest = jnp.concatenate(
            [one, pltpu.roll(one, 128 - own, 1), two, pltpu.roll(two, 128 - own, 1)], axis=0
        )
        halves.append(jnp.concatenate(rows + [rest], axis=1))
    for kz in range(3):
        low = (2 - kz) * own
        mine, other = (halves[h][low : low + own].T[:taps] for h in range(2))
        wgrad_ref[kz * taps : (kz + 1) * taps, :] = jnp.where(
            chan == 0,
            jnp.concatenate([mine, other], axis=1),
            jnp.concatenate([other, mine], axis=1),
        )
    decode(ZP - 1)

    @pl.when(has_below)
    def _():
        for copy in downward() + [far_down()]:
            copy.wait_send()

    @pl.when(has_above)
    def _():
        for copy in upward() + [far_up()]:
            copy.wait_send()

    for copy in part_copies + scale_copies + pair_copies:
        copy.wait_send()
    for h in range(2):
        for d in range(1, chips):
            chip_copy(h, d).wait_send()
            last_copy(h, d).wait_send()
        back_copy(h).wait_send()


def write_kernel(a_ref, b_ref, c_ref, a_out, b_out, c_out, sems):
    copies = [
        pltpu.make_async_copy(source, target, sems.at[k])
        for k, (source, target) in enumerate(((a_ref, a_out), (b_ref, b_out), (c_ref, c_out)))
    ]
    for copy in copies:
        copy.start()
    for copy in copies:
        copy.wait()


def fused_device(x_slab, weights, cotangent):
    every, own = weights.shape[0], weights.shape[1]
    height, width = x_slab.shape[3], x_slab.shape[4]
    cells = height * width
    tall = cells + 2 * width
    tiles = lax.axis_size("tile")
    chips = tiles // 2
    w_taps = weights.transpose(2, 1, 0).reshape(27 * own, every)
    taps = 9 * own
    rows = -(-(10 * own + own // 2) // (16 * chips)) * (16 * chips)
    scale = 1.0 / math.sqrt(ZP * cells * tiles)
    vmem = pl.BlockSpec(memory_space=pltpu.VMEM)
    dma = pltpu.SemaphoreType.DMA
    bf16, f32 = jnp.bfloat16, jnp.float32
    hbm = pl.BlockSpec(memory_space=pl.ANY)
    shapes = (
        ((own, ZP, height, width), bf16),
        ((own, ZP + 2, height, width), bf16),
        ((27 * own, every), f32),
    )
    held = pl.pallas_call(
        functools.partial(fused_kernel, (own, height, width, tiles, scale)),
        out_shape=tuple(pltpu.VMEM(*shape) for shape in shapes),
        in_specs=[hbm] * 3,
        out_specs=(vmem,) * 3,
        scratch_shapes=[
            pltpu.VMEM((own, ZP + 2, height, width), bf16),
            pltpu.VMEM((own, ZP, height, width), bf16),
            pltpu.VMEM((27 * own, every), bf16),
            dma((ZP + 2,)),
            pltpu.SemaphoreType.REGULAR(((tiles - 1).bit_length(),)),
            pltpu.VMEM((ZP + 2, own, tall), bf16),
            pltpu.VMEM((2, ZP, own, tall), bf16),
            pltpu.VMEM(((ZP + 2) * taps, cells), bf16),
            pltpu.VMEM((2, taps, cells), bf16),
            pltpu.VMEM((ZP + 2, own, cells), f32),
            pltpu.VMEM((3 * every, taps), bf16),
            pltpu.VMEM((2, 3 * own, taps), bf16),
            pltpu.VMEM((ZP, every, cells), f32),
            pltpu.VMEM((ZP, own, cells), bf16),
            pltpu.VMEM((ZP, own, cells), bf16),
            pltpu.VMEM((ZP, 8, 128), f32),
            pltpu.VMEM((ZP, 8, 128), f32),
            pltpu.VMEM((2, 3 * own, 512), f32),
            pltpu.VMEM((2, rows, 128), f32),
            pltpu.VMEM((2, rows // 2, 128), f32),
            pltpu.VMEM((2, chips - 1, rows // tiles, 128), f32),
            pltpu.VMEM((2, rows, 128), f32),
            dma((4,)),
            dma((4,)),
            dma((2,)),
            dma((2,)),
            dma((ZP,)),
            dma((ZP,)),
            dma((ZP,)),
            dma((ZP,)),
            dma((ZP,)),
            dma((ZP,)),
            dma((2,)),
            dma((2,)),
            dma((2, chips - 1)),
            dma((2, chips - 1)),
            dma((2, chips - 1)),
            dma((2, chips - 1)),
            dma((2,)),
            dma((2,)),
        ],
        compiler_params=pltpu.CompilerParams(
            vmem_limit_bytes=58 * 1024 * 1024, collective_id=0, has_side_effects=True
        ),
    )(x_slab[0], cotangent[0], w_taps)
    out_flat, in_flat, terms = pl.pallas_call(
        write_kernel,
        out_shape=tuple(jax.ShapeDtypeStruct(*shape) for shape in shapes),
        in_specs=[hbm] * 3,
        out_specs=(hbm,) * 3,
        scratch_shapes=[dma((3,))],
        compiler_params=pltpu.CompilerParams(vmem_limit_bytes=1024 * 1024),
    )(*(pltpu.with_memory_space_constraint(value, pltpu.VMEM) for value in held))
    weight_grad = terms.reshape(27, own, every).transpose(2, 1, 0)
    return (out_flat[None], in_flat[None], weight_grad)


def solution(mesh):
    in_specs = (
        P("tile", "chan", None, None, None),
        P(None, "chan", None),
        P("tile", "chan", None, None, None),
    )
    out_specs = (
        P("tile", "chan", None, None, None),
        P("tile", "chan", None, None, None),
        P(None, "chan", None),
    )
    fused = mesh.shape["chan"] == 2 and mesh.shape["tile"] == 16
    return jax.shard_map(
        fused_device if fused else per_device, mesh=mesh, in_specs=in_specs, out_specs=out_specs, check_vma=False
    )
```

```python
import functools
import math

import jax
import jax.numpy as jnp
from jax import lax
from jax.experimental import pallas as pl
from jax.experimental.pallas import tpu as pltpu
from jax.sharding import PartitionSpec as P

ZP = 4


def shifted(value, axis, steps):
    count = lax.axis_size(axis)
    initial, last = (max(0, -steps), min(count, count - steps))
    return lax.ppermute(value, axis, [(source, source + steps) for source in range(initial, last)])


def with_rims(cells, width):
    above = shifted(cells[:, :, -width:], "tile", 1)
    below = shifted(cells[:, :, :width], "tile", -1)
    return jnp.concatenate([above, cells, below], axis=-1)


def tap_copies(tall, width):
    wide = tall.astype(jnp.float32)
    lanes = wide.shape[1]
    col = lax.broadcasted_iota(jnp.int32, wide.shape, 1) % width
    left = jnp.where(col == 0, 0.0, pltpu.roll(wide, 1, 1)).astype(jnp.bfloat16)
    right = jnp.where(col == width - 1, 0.0, pltpu.roll(wide, lanes - 1, 1)).astype(jnp.bfloat16)
    return left, tall, right


def conv_kernel(
    dims, xe_ref, de_ref, wout_ref, win_ref, part_ref, ingrad_ref, wgrad_ref, x9, d9, acc
):
    own, every, height, width = dims
    cells = height * width
    chunk = 2 * width

    def build_x(p, carry):
        copies = tap_copies(xe_ref[p], width)
        for ky in range(3):
            for kx in range(3):
                at = pl.multiple_of(p * (9 * own) + (3 * ky + kx) * own, 16)
                x9[pl.ds(at, own), :] = copies[kx][:, ky * width : ky * width + cells]
        return carry

    lax.fori_loop(0, ZP + 2, build_x, 0)

    def forward(step, carry):
        z = step // (cells // chunk)
        at = pl.multiple_of((step % (cells // chunk)) * chunk, chunk)
        rows = pl.ds(pl.multiple_of(z * (9 * own), 16), 27 * own)
        part_ref[z, :, pl.ds(at, chunk)] = jnp.dot(
            wout_ref[...], x9[rows, pl.ds(at, chunk)], preferred_element_type=jnp.float32
        )
        return carry

    lax.fori_loop(0, ZP * (cells // chunk), forward, 0)

    acc[...] = jnp.zeros_like(acc)

    def backward(p, carry):
        copies = tap_copies(de_ref[p], width)
        for ky in range(3):
            for kx in range(3):
                at = (3 * ky + kx) * every
                d9[at : at + every, :] = copies[kx][:, ky * width : ky * width + cells]

        def part(j, inner):
            at = pl.multiple_of(j * chunk, chunk)
            product = jnp.dot(
                win_ref[...], d9[:, pl.ds(at, chunk)], preferred_element_type=jnp.float32
            )
            for kz in range(3):
                acc[p + kz, :, pl.ds(at, chunk)] += product[kz * own : (kz + 1) * own]
            return inner

        return lax.fori_loop(0, cells // chunk, part, carry)

    lax.fori_loop(0, ZP, backward, 0)
    ingrad_ref[...] = acc[...].astype(jnp.bfloat16)

    wgrad_ref[...] = jnp.zeros_like(wgrad_ref)

    def kernel_terms(step, carry):
        z, kz = step // 3, step % 3
        rows = pl.ds(pl.multiple_of((z + kz) * (9 * own), 16), 9 * own)
        wgrad_ref[kz] += lax.dot_general(
            de_ref[z, :, width : width + cells],
            x9[rows, :],
            (((1,), (1,)), ((), ())),
            preferred_element_type=jnp.float32,
        )
        return carry

    lax.fori_loop(0, ZP * 3, kernel_terms, 0)


def per_device(x_slab, weights, cotangent):
    every, own_real = weights.shape[0], weights.shape[1]
    own = -(-own_real // 16) * 16
    height, width = x_slab.shape[3], x_slab.shape[4]
    cells = height * width
    spare = own - own_real
    flat_x = x_slab[0].transpose(1, 0, 2, 3).reshape(ZP + 2, own_real, cells)
    flat_dy = cotangent[0].transpose(1, 0, 2, 3).reshape(ZP, own_real, cells)
    dy_all = lax.all_gather(flat_dy, "chan", axis=1, tiled=True)
    x_rims = with_rims(flat_x, width)
    d_rims = with_rims(dy_all, width)
    if spare:
        x_rims = jnp.pad(x_rims, ((0, 0), (0, spare), (0, 0)))
        weights = jnp.pad(weights, ((0, 0), (0, spare), (0, 0)))
    w_out = weights.transpose(0, 2, 1).reshape(every, 27 * own)
    w_in = (
        weights.reshape(every, own, 3, 9)[:, :, :, ::-1]
        .transpose(2, 1, 3, 0)
        .reshape(3 * own, 9 * every)
    )
    vmem = pl.BlockSpec(memory_space=pltpu.VMEM)
    part, in_flat, terms = pl.pallas_call(
        functools.partial(conv_kernel, (own, every, height, width)),
        out_shape=(
            jax.ShapeDtypeStruct((ZP, every, cells), jnp.float32),
            jax.ShapeDtypeStruct((ZP + 2, own, cells), jnp.bfloat16),
            jax.ShapeDtypeStruct((3, every, 9 * own), jnp.float32),
        ),
        in_specs=[vmem] * 4,
        out_specs=(vmem,) * 3,
        scratch_shapes=[
            pltpu.VMEM(((ZP + 2) * 9 * own, cells), jnp.bfloat16),
            pltpu.VMEM((9 * every, cells), jnp.bfloat16),
            pltpu.VMEM((ZP + 2, own, cells), jnp.float32),
        ],
        compiler_params=pltpu.CompilerParams(vmem_limit_bytes=48 * 1024 * 1024),
    )(x_rims, d_rims, w_out, w_in)
    total = lax.psum_scatter(part, "chan", scatter_dimension=1, tiled=True)
    out_field = (
        total.astype(jnp.bfloat16)
        .reshape(ZP, own_real, height, width)
        .transpose(1, 0, 2, 3)[None]
    )
    in_grad = (
        in_flat[:, :own_real].reshape(ZP + 2, own_real, height, width).transpose(1, 0, 2, 3)[None]
    )
    scale = 1.0 / math.sqrt(ZP * cells * lax.axis_size("tile"))
    summed = lax.psum(terms, "tile") * scale
    weight_grad = (
        summed.reshape(3, every, 9, own)[..., :own_real]
        .transpose(1, 3, 0, 2)
        .reshape(every, own_real, 27)
    )
    return (out_field, in_grad, weight_grad)


LEVELS = 250.0
BEND = 3.0


def row_codes(value, inverse):
    ratio = jnp.abs(value) * inverse
    bent = ratio * (1.0 + BEND) / (1.0 + BEND * ratio)
    size = jnp.exp2(bent * LEVELS - 0.5 * LEVELS)
    return jnp.where(value < 0.0, -size, size).astype(jnp.bfloat16)


def row_values(codes, largest):
    wide = codes.astype(jnp.float32)
    bent = jnp.log2(jnp.abs(wide)) * (1.0 / LEVELS) + 0.5
    size = bent * largest / ((1.0 + BEND) - BEND * bent)
    return jnp.where(wide < 0.0, -size, size)


def diagonal(count):
    shape = (count, 128)
    return lax.broadcasted_iota(jnp.int32, shape, 0) == lax.broadcasted_iota(jnp.int32, shape, 1)


def fused_kernel(
    dims,
    x_hbm,
    dy_hbm,
    w_hbm,
    out_ref,
    ingrad_ref,
    wgrad_ref,
    x_ref,
    dy_ref,
    w_ref,
    load_sem,
    entered,
    xe,
    de,
    x9,
    d9,
    acc,
    wout,
    win,
    both,
    coded,
    incoming,
    scale_out,
    scale_in,
    sums,
    terms,
    pair_in,
    chip_in,
    final,
    rim_send,
    rim_recv,
    far_send,
    far_recv,
    dy_send,
    dy_recv,
    part_send,
    part_recv,
    scale_send,
    scale_recv,
    pair_send,
    pair_recv,
    chip_send,
    chip_recv,
    last_send,
    last_recv,
    back_send,
    back_recv,
):
    own, height, width, tiles, scale = dims
    every = 2 * own
    taps = 9 * own
    cells = height * width
    tall = cells + 2 * width
    tile, chan = lax.axis_index("tile"), lax.axis_index("chan")
    core, chip, chips = tile % 2, tile // 2, tiles // 2
    half_rows = terms.shape[1] // 2
    piece = half_rows // chips
    f32, bf16 = jnp.float32, jnp.bfloat16

    def there(t, c):
        return {"tile": t, "chan": c}

    def remote(src, dst, send, recv, to):
        return pltpu.make_async_remote_copy(
            src_ref=src,
            dst_ref=dst,
            send_sem=send,
            recv_sem=recv,
            device_id=to,
            device_id_type=pl.DeviceIdType.MESH,
        )

    barrier = pltpu.get_barrier_semaphore()

    def greet(to):
        pl.semaphore_signal(barrier, inc=1, device_id=to, device_id_type=pl.DeviceIdType.MESH)

    has_above, has_below = tile > 0, tile < tiles - 1
    greet(there(tile, 1 - chan))

    @pl.when(has_above)
    def _():
        greet(there(tile - 1, chan))

    @pl.when(has_below)
    def _():
        greet(there(tile + 1, chan))

    loads = [
        pltpu.make_async_copy(source, target, load_sem.at[k])
        for k, (source, target) in enumerate(
            [(dy_hbm.at[:, p], dy_ref.at[:, p]) for p in range(ZP)]
            + [(x_hbm, x_ref), (w_hbm, w_ref)]
        )
    ]
    for load in loads:
        load.start()
    middle = pl.ds(width, cells)
    partner = there(tile, 1 - chan)
    dy_copies = [
        remote(de.at[0, p, :, middle], de.at[1, p, :, middle], dy_send.at[p], dy_recv.at[p], partner)
        for p in range(ZP)
    ]
    for p in range(ZP):
        loads[p].wait()
        de[0, p, :, width : width + cells] = dy_ref[:, p].reshape(own, cells)
        if p == 0:
            expected = 1 + jnp.where(has_above, 1, 0) + jnp.where(has_below, 1, 0)
            pl.semaphore_wait(barrier, expected)
        dy_copies[p].start()
    loads[ZP].wait()
    for p in range(ZP + 2):
        xe[p, :, width : width + cells] = x_ref[:, p].reshape(own, cells)

    @pl.when(tile == 0)
    def _():
        xe[:, :, 0:width] = jnp.zeros((ZP + 2, own, width), bf16)
        de[:, :, :, 0:width] = jnp.zeros((2, ZP, own, width), bf16)

    @pl.when(tile == tiles - 1)
    def _():
        xe[:, :, cells + width : tall] = jnp.zeros((ZP + 2, own, width), bf16)
        de[:, :, :, cells + width : tall] = jnp.zeros((2, ZP, own, width), bf16)

    top, bottom = pl.ds(width, width), pl.ds(cells, width)
    rim_top, rim_bottom = pl.ds(0, width), pl.ds(cells + width, width)

    def rim_copies(to, src_lanes, dst_lanes, at):
        return [
            remote(xe.at[:, :, src_lanes], xe.at[:, :, dst_lanes],
                   rim_send.at[at], rim_recv.at[at], there(to, chan)),
            remote(de.at[0, :, :, src_lanes], de.at[0, :, :, dst_lanes],
                   rim_send.at[at + 1], rim_recv.at[at + 1], there(to, chan)),
        ]

    def downward():
        return rim_copies(tile + 1, bottom, rim_top, 0)

    def upward():
        return rim_copies(tile - 1, top, rim_bottom, 2)

    def far_down():
        return remote(de.at[1, :, :, bottom], de.at[1, :, :, rim_top],
                      far_send.at[0], far_recv.at[0], there(tile + 1, chan))

    def far_up():
        return remote(de.at[1, :, :, top], de.at[1, :, :, rim_bottom],
                      far_send.at[1], far_recv.at[1], there(tile - 1, chan))

    @pl.when(has_below)
    def _():
        for copy in downward():
            copy.start()

    @pl.when(has_above)
    def _():
        for copy in upward():
            copy.start()

    def tell(k):
        step = 2**k

        @pl.when(tile >= step)
        def _():
            pl.semaphore_signal(entered.at[k], inc=1, device_id=there(tile - step, chan),
                                device_id_type=pl.DeviceIdType.MESH)

        @pl.when(tile < tiles - step)
        def _():
            pl.semaphore_signal(entered.at[k], inc=1, device_id=there(tile + step, chan),
                                device_id_type=pl.DeviceIdType.MESH)

    def hear(k):
        step = 2**k
        pl.semaphore_wait(
            entered.at[k], jnp.where(tile >= step, 1, 0) + jnp.where(tile < tiles - step, 1, 0)
        )

    rounds = (tiles - 1).bit_length()
    tell(0)

    loads[ZP + 1].wait()
    whole = w_ref[...].astype(f32)
    swapped = jnp.concatenate([whole[:, own:], whole[:, :own]], axis=1)
    ordered = jnp.where(chan == 0, whole, swapped)
    for kz in range(3):
        wout[(2 - kz) * every : (3 - kz) * every, :] = (
            ordered[kz * taps : (kz + 1) * taps].T.astype(bf16)
        )
    ordered = ordered.astype(bf16)
    for kz in range(3):
        for r in range(9):
            at = (kz * 9 + 8 - r) * own
            for h in range(2):
                win[h, kz * own : (kz + 1) * own, r * own : (r + 1) * own] = (
                    ordered[at : at + own, h * own : (h + 1) * own]
                )


    @pl.when(has_above)
    def _():
        for copy in downward():
            copy.wait_recv()

    @pl.when(has_below)
    def _():
        for copy in upward():
            copy.wait_recv()

    part_copies = [
        remote(coded.at[z], incoming.at[z], part_send.at[z], part_recv.at[z], partner)
        for z in range(ZP)
    ]
    scale_copies = [
        remote(scale_out.at[z], scale_in.at[z], scale_send.at[z], scale_recv.at[z], partner)
        for z in range(ZP)
    ]
    diag = diagonal(own)
    chunk = 2 * width

    def encode(z):
        lanes = jnp.zeros((own, 128), f32)
        for at in range(0, cells, 128):
            lanes = jnp.maximum(lanes, jnp.abs(both[z, own:every, at : at + 128]))
        largest = jnp.maximum(jnp.max(lanes, axis=1, keepdims=True), 1e-30)
        spread = jnp.sum(jnp.where(diag, largest, 0.0), axis=0, keepdims=True)
        scale_out[z] = spread
        inverse = 1.0 / largest
        for at in range(0, cells, chunk):
            coded[z, :, at : at + chunk] = row_codes(both[z, own:every, at : at + chunk], inverse)

    def build(value, target, at):
        copies = tap_copies(value, width)
        for ky in range(3):
            for kx in range(3):
                row = at + (3 * ky + kx) * own
                target[row : row + own, :] = copies[kx][:, ky * width : ky * width + cells]

    def planes_of(p):
        return max(0, p - 2), min(ZP - 1, p)

    for p in range(ZP + 2):
        build(xe[p], x9, p * taps)
        first, last = planes_of(p)
        low = (first - p + 2) * every
        product = jnp.dot(
            wout[low : low + (last - first + 1) * every, :],
            x9[p * taps : (p + 1) * taps, :],
            preferred_element_type=f32,
        )
        for z in range(first, last + 1):
            block = product[(z - first) * every : (z - first + 1) * every]
            if z == p:
                both[z] = block
            else:
                both[z] += block
        if p >= 2:
            encode(p - 2)
        if p in (1, 4) and p // 3 + 1 < rounds:
            hear(p // 3)
            tell(p // 3 + 1)

    def kernel_terms(h):
        for p in range(ZP + 2):
            first, last = planes_of(p)
            count = last - first + 1
            if h == 1 and p == 0:
                for copy in dy_copies[: ZP - 1]:
                    copy.wait_recv()
            if h == 1 and p == ZP - 1:
                dy_copies[p].wait_recv()

                @pl.when(has_below)
                def _():
                    far_down().start()

                @pl.when(has_above)
                def _():
                    far_up().start()

            value = lax.dot_general(
                de[h, first : last + 1, :, width : width + cells].reshape(count * own, cells),
                x9[p * taps : (p + 1) * taps, :],
                (((1,), (1,)), ((), ())),
                preferred_element_type=f32,
            )
            low = (first - p + 2) * own
            if p == 0:
                sums[h] = jnp.zeros_like(sums[h])
            sums[h, low : low + count * own, 0:taps] += value
        for q in range(3):
            terms[h, q * 3 * own : (q + 1) * 3 * own, :] = sums[h, :, q * 128 : (q + 1) * 128]
        rest = sums[h, :, 384:512]
        lane = lax.broadcasted_iota(jnp.int32, (own, 128), 1)
        packed = jnp.where(lane < own, rest[0:own], pltpu.roll(rest[own : 2 * own], own, 1))
        terms[h, 9 * own : 10 * own, :] = packed
        lane = lax.broadcasted_iota(jnp.int32, (own // 2, 128), 1)
        lower, upper = rest[2 * own : 2 * own + own // 2], rest[2 * own + own // 2 :]
        packed = jnp.where(lane < own, lower, pltpu.roll(upper, own, 1))
        terms[h, 10 * own : 10 * own + own // 2, :] = packed
        left = terms.shape[1] - (10 * own + own // 2)
        terms[h, 10 * own + own // 2 :, :] = jnp.zeros((left, 128), f32)

    keep_at = pl.multiple_of(core * half_rows, 8)
    give_at = pl.multiple_of((1 - core) * half_rows, 8)
    keep, give = pl.ds(keep_at, half_rows), pl.ds(give_at, half_rows)
    neighbour = there(chip * 2 + 1 - core, chan)

    def piece_of(index):
        return pl.ds(pl.multiple_of(keep_at + index * piece, 8), piece)

    pair_copies = [
        remote(terms.at[h, give, :], pair_in.at[h], pair_send.at[h], pair_recv.at[h], neighbour)
        for h in range(2)
    ]

    def chip_copy(h, d):
        to = (chip + d) % chips
        return remote(terms.at[h, piece_of(to), :], chip_in.at[h, d - 1],
                      chip_send.at[h, d - 1], chip_recv.at[h, d - 1], there(to * 2 + core, chan))

    def last_copy(h, d):
        to = (chip + d) % chips
        return remote(final.at[h, piece_of(chip), :], final.at[h, piece_of(chip), :],
                      last_send.at[h, d - 1], last_recv.at[h, d - 1], there(to * 2 + core, chan))

    def last_arrival(h, d):
        source = (chip + chips - d) % chips
        return remote(final.at[h, piece_of(source), :], final.at[h, piece_of(source), :],
                      last_send.at[h, d - 1], last_recv.at[h, d - 1],
                      there(source * 2 + core, chan))

    def back_copy(h):
        return remote(final.at[h, keep, :], final.at[h, keep, :],
                      back_send.at[h], back_recv.at[h], neighbour)

    def back_arrival(h):
        return remote(final.at[h, give, :], final.at[h, give, :],
                      back_send.at[h], back_recv.at[h], neighbour)

    def to_chips(h):
        pair_copies[h].wait_recv()
        terms[h, keep, :] += pair_in[h]
        for d in range(1, chips):
            chip_copy(h, d).start()

    def from_chips(h):
        total = terms[h, piece_of(chip), :]
        for d in range(1, chips):
            chip_copy(h, d).wait_recv()
            total += chip_in[h, d - 1]
        final[h, piece_of(chip), :] = total * scale
        for d in range(1, chips):
            last_copy(h, d).start()

    def to_pair(h):
        for d in range(1, chips):
            last_arrival(h, d).wait_recv()
        back_copy(h).start()

    def backward(h, p):
        build(de[h, p], d9.at[p % 2], 0)
        product = jnp.dot(win[h], d9[p % 2], preferred_element_type=f32)
        for kz in range(3):
            block = product[kz * own : (kz + 1) * own]
            if h == 0 and (p == 0 or kz == 2):
                acc[p + kz] = block
            else:
                acc[p + kz] += block

    kernel_terms(0)
    pair_copies[0].start()
    for k in range(2, min(3, rounds)):
        hear(k)
        if k + 1 < rounds:
            tell(k + 1)
    for p in range(ZP):
        backward(0, p)
    for k in range(3, rounds):
        hear(k)
        if k + 1 < rounds:
            tell(k + 1)
    to_chips(0)

    for copy in dy_copies:
        copy.wait_send()
    for z in range(ZP):
        scale_copies[z].start()
        part_copies[z].start()
    kernel_terms(1)
    pair_copies[1].start()
    from_chips(0)

    @pl.when(has_above)
    def _():
        far_down().wait_recv()

    @pl.when(has_below)
    def _():
        far_up().wait_recv()

    def finish(s):
        ingrad_ref[:, s] = acc[s].reshape(own, height, width).astype(bf16)

    to_chips(1)
    backward(1, 0)
    finish(0)
    for p in range(1, ZP):
        backward(1, p)
        finish(p)
    finish(ZP)
    finish(ZP + 1)
    to_pair(0)

    def decode(z):
        scale_copies[z].wait_recv()
        part_copies[z].wait_recv()
        row = jnp.broadcast_to(scale_in[z], (own, 128))
        largest = jnp.sum(jnp.where(diag, row, 0.0), axis=1, keepdims=True)
        for at in range(0, cells, chunk):
            total = both[z, 0:own, at : at + chunk] + row_values(
                incoming[z, :, at : at + chunk], largest
            )
            lines = slice(at // width, (at + chunk) // width)
            out_ref[:, z, lines] = total.reshape(own, chunk // width, width).astype(bf16)

    def turned(h):
        back_arrival(h).wait_recv()
        rows = [final[h, q * 3 * own : (q + 1) * 3 * own, :] for q in range(3)]
        one = final[h, 9 * own : 10 * own, :]
        two = final[h, 10 * own : 10 * own + own // 2, :]
        rest = jnp.concatenate(
            [one, pltpu.roll(one, 128 - own, 1), two, pltpu.roll(two, 128 - own, 1)], axis=0
        )
        half = jnp.concatenate(rows + [rest], axis=1)
        return [half[(2 - kz) * own : (3 - kz) * own].T[:taps] for kz in range(3)]

    from_chips(1)
    decode(0)
    mines = turned(0)
    decode(1)
    to_pair(1)
    decode(2)

    others = turned(1)
    for kz in range(3):
        mine, other = mines[kz], others[kz]
        wgrad_ref[kz * taps : (kz + 1) * taps, :] = jnp.where(
            chan == 0,
            jnp.concatenate([mine, other], axis=1),
            jnp.concatenate([other, mine], axis=1),
        )
    decode(ZP - 1)

    @pl.when(has_below)
    def _():
        for copy in downward() + [far_down()]:
            copy.wait_send()

    @pl.when(has_above)
    def _():
        for copy in upward() + [far_up()]:
            copy.wait_send()

    for copy in part_copies + scale_copies + pair_copies:
        copy.wait_send()
    for h in range(2):
        for d in range(1, chips):
            chip_copy(h, d).wait_send()
            last_copy(h, d).wait_send()
        back_copy(h).wait_send()


def write_kernel(a_ref, b_ref, c_ref, a_out, b_out, c_out, sems):
    copies = [
        pltpu.make_async_copy(source, target, sems.at[k])
        for k, (source, target) in enumerate(((a_ref, a_out), (b_ref, b_out), (c_ref, c_out)))
    ]
    for copy in copies:
        copy.start()
    for copy in copies:
        copy.wait()


def fused_device(x_slab, weights, cotangent):
    every, own = weights.shape[0], weights.shape[1]
    height, width = x_slab.shape[3], x_slab.shape[4]
    cells = height * width
    tall = cells + 2 * width
    tiles = lax.axis_size("tile")
    chips = tiles // 2
    w_taps = weights.transpose(2, 1, 0).reshape(27 * own, every)
    taps = 9 * own
    rows = -(-(10 * own + own // 2) // (16 * chips)) * (16 * chips)
    scale = 1.0 / math.sqrt(ZP * cells * tiles)
    vmem = pl.BlockSpec(memory_space=pltpu.VMEM)
    dma = pltpu.SemaphoreType.DMA
    bf16, f32 = jnp.bfloat16, jnp.float32
    hbm = pl.BlockSpec(memory_space=pl.ANY)
    shapes = (
        ((own, ZP, height, width), bf16),
        ((own, ZP + 2, height, width), bf16),
        ((27 * own, every), f32),
    )
    held = pl.pallas_call(
        functools.partial(fused_kernel, (own, height, width, tiles, scale)),
        out_shape=tuple(pltpu.VMEM(*shape) for shape in shapes),
        in_specs=[hbm] * 3,
        out_specs=(vmem,) * 3,
        scratch_shapes=[
            pltpu.VMEM((own, ZP + 2, height, width), bf16),
            pltpu.VMEM((own, ZP, height, width), bf16),
            pltpu.VMEM((27 * own, every), bf16),
            dma((ZP + 2,)),
            pltpu.SemaphoreType.REGULAR(((tiles - 1).bit_length(),)),
            pltpu.VMEM((ZP + 2, own, tall), bf16),
            pltpu.VMEM((2, ZP, own, tall), bf16),
            pltpu.VMEM(((ZP + 2) * taps, cells), bf16),
            pltpu.VMEM((2, taps, cells), bf16),
            pltpu.VMEM((ZP + 2, own, cells), f32),
            pltpu.VMEM((3 * every, taps), bf16),
            pltpu.VMEM((2, 3 * own, taps), bf16),
            pltpu.VMEM((ZP, every, cells), f32),
            pltpu.VMEM((ZP, own, cells), bf16),
            pltpu.VMEM((ZP, own, cells), bf16),
            pltpu.VMEM((ZP, 1, 128), f32),
            pltpu.VMEM((ZP, 1, 128), f32),
            pltpu.VMEM((2, 3 * own, 512), f32),
            pltpu.VMEM((2, rows, 128), f32),
            pltpu.VMEM((2, rows // 2, 128), f32),
            pltpu.VMEM((2, chips - 1, rows // tiles, 128), f32),
            pltpu.VMEM((2, rows, 128), f32),
            dma((4,)),
            dma((4,)),
            dma((2,)),
            dma((2,)),
            dma((ZP,)),
            dma((ZP,)),
            dma((ZP,)),
            dma((ZP,)),
            dma((ZP,)),
            dma((ZP,)),
            dma((2,)),
            dma((2,)),
            dma((2, chips - 1)),
            dma((2, chips - 1)),
            dma((2, chips - 1)),
            dma((2, chips - 1)),
            dma((2,)),
            dma((2,)),
        ],
        compiler_params=pltpu.CompilerParams(
            vmem_limit_bytes=58 * 1024 * 1024, collective_id=0, has_side_effects=True
        ),
    )(x_slab[0], cotangent[0], w_taps)
    out_flat, in_flat, terms = pl.pallas_call(
        write_kernel,
        out_shape=tuple(jax.ShapeDtypeStruct(*shape) for shape in shapes),
        in_specs=[hbm] * 3,
        out_specs=(hbm,) * 3,
        scratch_shapes=[dma((3,))],
        compiler_params=pltpu.CompilerParams(vmem_limit_bytes=1024 * 1024),
    )(*(pltpu.with_memory_space_constraint(value, pltpu.VMEM) for value in held))
    weight_grad = terms.reshape(27, own, every).transpose(2, 1, 0)
    return (out_flat[None], in_flat[None], weight_grad)


def solution(mesh):
    in_specs = (
        P("tile", "chan", None, None, None),
        P(None, "chan", None),
        P("tile", "chan", None, None, None),
    )
    out_specs = (
        P("tile", "chan", None, None, None),
        P("tile", "chan", None, None, None),
        P(None, "chan", None),
    )
    fused = mesh.shape["chan"] == 2 and mesh.shape["tile"] == 16
    return jax.shard_map(
        fused_device if fused else per_device, mesh=mesh, in_specs=in_specs, out_specs=out_specs, check_vma=False
    )
```

```python
import functools
import math

import jax
import jax.numpy as jnp
from jax import lax
from jax.experimental import pallas as pl
from jax.experimental.pallas import tpu as pltpu
from jax.sharding import PartitionSpec as P

ZP = 4


def shifted(value, axis, steps):
    count = lax.axis_size(axis)
    initial, last = (max(0, -steps), min(count, count - steps))
    return lax.ppermute(value, axis, [(source, source + steps) for source in range(initial, last)])


def with_rims(cells, width):
    above = shifted(cells[:, :, -width:], "tile", 1)
    below = shifted(cells[:, :, :width], "tile", -1)
    return jnp.concatenate([above, cells, below], axis=-1)


def tap_copies(tall, width):
    wide = tall.astype(jnp.float32)
    lanes = wide.shape[1]
    col = lax.broadcasted_iota(jnp.int32, wide.shape, 1) % width
    left = jnp.where(col == 0, 0.0, pltpu.roll(wide, 1, 1)).astype(jnp.bfloat16)
    right = jnp.where(col == width - 1, 0.0, pltpu.roll(wide, lanes - 1, 1)).astype(jnp.bfloat16)
    return left, tall, right


def conv_kernel(
    dims, xe_ref, de_ref, wout_ref, win_ref, part_ref, ingrad_ref, wgrad_ref, x9, d9, acc
):
    own, every, height, width = dims
    cells = height * width
    chunk = 2 * width

    def build_x(p, carry):
        copies = tap_copies(xe_ref[p], width)
        for ky in range(3):
            for kx in range(3):
                at = pl.multiple_of(p * (9 * own) + (3 * ky + kx) * own, 16)
                x9[pl.ds(at, own), :] = copies[kx][:, ky * width : ky * width + cells]
        return carry

    lax.fori_loop(0, ZP + 2, build_x, 0)

    def forward(step, carry):
        z = step // (cells // chunk)
        at = pl.multiple_of((step % (cells // chunk)) * chunk, chunk)
        rows = pl.ds(pl.multiple_of(z * (9 * own), 16), 27 * own)
        part_ref[z, :, pl.ds(at, chunk)] = jnp.dot(
            wout_ref[...], x9[rows, pl.ds(at, chunk)], preferred_element_type=jnp.float32
        )
        return carry

    lax.fori_loop(0, ZP * (cells // chunk), forward, 0)

    acc[...] = jnp.zeros_like(acc)

    def backward(p, carry):
        copies = tap_copies(de_ref[p], width)
        for ky in range(3):
            for kx in range(3):
                at = (3 * ky + kx) * every
                d9[at : at + every, :] = copies[kx][:, ky * width : ky * width + cells]

        def part(j, inner):
            at = pl.multiple_of(j * chunk, chunk)
            product = jnp.dot(
                win_ref[...], d9[:, pl.ds(at, chunk)], preferred_element_type=jnp.float32
            )
            for kz in range(3):
                acc[p + kz, :, pl.ds(at, chunk)] += product[kz * own : (kz + 1) * own]
            return inner

        return lax.fori_loop(0, cells // chunk, part, carry)

    lax.fori_loop(0, ZP, backward, 0)
    ingrad_ref[...] = acc[...].astype(jnp.bfloat16)

    wgrad_ref[...] = jnp.zeros_like(wgrad_ref)

    def kernel_terms(step, carry):
        z, kz = step // 3, step % 3
        rows = pl.ds(pl.multiple_of((z + kz) * (9 * own), 16), 9 * own)
        wgrad_ref[kz] += lax.dot_general(
            de_ref[z, :, width : width + cells],
            x9[rows, :],
            (((1,), (1,)), ((), ())),
            preferred_element_type=jnp.float32,
        )
        return carry

    lax.fori_loop(0, ZP * 3, kernel_terms, 0)


def per_device(x_slab, weights, cotangent):
    every, own_real = weights.shape[0], weights.shape[1]
    own = -(-own_real // 16) * 16
    height, width = x_slab.shape[3], x_slab.shape[4]
    cells = height * width
    spare = own - own_real
    flat_x = x_slab[0].transpose(1, 0, 2, 3).reshape(ZP + 2, own_real, cells)
    flat_dy = cotangent[0].transpose(1, 0, 2, 3).reshape(ZP, own_real, cells)
    dy_all = lax.all_gather(flat_dy, "chan", axis=1, tiled=True)
    x_rims = with_rims(flat_x, width)
    d_rims = with_rims(dy_all, width)
    if spare:
        x_rims = jnp.pad(x_rims, ((0, 0), (0, spare), (0, 0)))
        weights = jnp.pad(weights, ((0, 0), (0, spare), (0, 0)))
    w_out = weights.transpose(0, 2, 1).reshape(every, 27 * own)
    w_in = (
        weights.reshape(every, own, 3, 9)[:, :, :, ::-1]
        .transpose(2, 1, 3, 0)
        .reshape(3 * own, 9 * every)
    )
    vmem = pl.BlockSpec(memory_space=pltpu.VMEM)
    part, in_flat, terms = pl.pallas_call(
        functools.partial(conv_kernel, (own, every, height, width)),
        out_shape=(
            jax.ShapeDtypeStruct((ZP, every, cells), jnp.float32),
            jax.ShapeDtypeStruct((ZP + 2, own, cells), jnp.bfloat16),
            jax.ShapeDtypeStruct((3, every, 9 * own), jnp.float32),
        ),
        in_specs=[vmem] * 4,
        out_specs=(vmem,) * 3,
        scratch_shapes=[
            pltpu.VMEM(((ZP + 2) * 9 * own, cells), jnp.bfloat16),
            pltpu.VMEM((9 * every, cells), jnp.bfloat16),
            pltpu.VMEM((ZP + 2, own, cells), jnp.float32),
        ],
        compiler_params=pltpu.CompilerParams(vmem_limit_bytes=48 * 1024 * 1024),
    )(x_rims, d_rims, w_out, w_in)
    total = lax.psum_scatter(part, "chan", scatter_dimension=1, tiled=True)
    out_field = (
        total.astype(jnp.bfloat16)
        .reshape(ZP, own_real, height, width)
        .transpose(1, 0, 2, 3)[None]
    )
    in_grad = (
        in_flat[:, :own_real].reshape(ZP + 2, own_real, height, width).transpose(1, 0, 2, 3)[None]
    )
    scale = 1.0 / math.sqrt(ZP * cells * lax.axis_size("tile"))
    summed = lax.psum(terms, "tile") * scale
    weight_grad = (
        summed.reshape(3, every, 9, own)[..., :own_real]
        .transpose(1, 3, 0, 2)
        .reshape(every, own_real, 27)
    )
    return (out_field, in_grad, weight_grad)


LEVELS = 250.0
BEND = 3.0


def row_codes(value, inverse):
    ratio = jnp.abs(value) * inverse
    bent = ratio * (1.0 + BEND) / (1.0 + BEND * ratio)
    size = jnp.exp2(bent * LEVELS - 0.5 * LEVELS)
    return jnp.where(value < 0.0, -size, size).astype(jnp.bfloat16)


def row_values(codes, largest):
    wide = codes.astype(jnp.float32)
    bent = jnp.log2(jnp.abs(wide)) * (1.0 / LEVELS) + 0.5
    size = bent * largest / ((1.0 + BEND) - BEND * bent)
    return jnp.where(wide < 0.0, -size, size)


def diagonal(count):
    shape = (count, 128)
    return lax.broadcasted_iota(jnp.int32, shape, 0) == lax.broadcasted_iota(jnp.int32, shape, 1)


def fused_kernel(
    dims,
    x_hbm,
    dy_hbm,
    w_hbm,
    out_ref,
    ingrad_ref,
    wgrad_ref,
    x_ref,
    dy_ref,
    w_ref,
    load_sem,
    entered,
    xe,
    de,
    x9,
    d9,
    acc,
    wout,
    win,
    both,
    coded,
    incoming,
    scale_out,
    scale_in,
    sums,
    terms,
    pair_in,
    chip_in,
    final,
    rim_send,
    rim_recv,
    far_send,
    far_recv,
    dy_send,
    dy_recv,
    part_send,
    part_recv,
    scale_send,
    scale_recv,
    pair_send,
    pair_recv,
    chip_send,
    chip_recv,
    last_send,
    last_recv,
    back_send,
    back_recv,
):
    own, height, width, tiles, scale = dims
    every = 2 * own
    taps = 9 * own
    cells = height * width
    tall = cells + 2 * width
    tile, chan = lax.axis_index("tile"), lax.axis_index("chan")
    core, chip, chips = tile % 2, tile // 2, tiles // 2
    half_rows = terms.shape[1] // 2
    piece = half_rows // chips
    f32, bf16 = jnp.float32, jnp.bfloat16

    def there(t, c):
        return {"tile": t, "chan": c}

    def remote(src, dst, send, recv, to):
        return pltpu.make_async_remote_copy(
            src_ref=src,
            dst_ref=dst,
            send_sem=send,
            recv_sem=recv,
            device_id=to,
            device_id_type=pl.DeviceIdType.MESH,
        )

    barrier = pltpu.get_barrier_semaphore()

    def greet(to):
        pl.semaphore_signal(barrier, inc=1, device_id=to, device_id_type=pl.DeviceIdType.MESH)

    has_above, has_below = tile > 0, tile < tiles - 1
    greet(there(tile, 1 - chan))

    @pl.when(has_above)
    def _():
        greet(there(tile - 1, chan))

    @pl.when(has_below)
    def _():
        greet(there(tile + 1, chan))

    loads = [
        pltpu.make_async_copy(source, target, load_sem.at[k])
        for k, (source, target) in enumerate(
            [(dy_hbm.at[:, p], dy_ref.at[:, p]) for p in range(ZP)]
            + [(x_hbm, x_ref), (w_hbm, w_ref)]
        )
    ]
    for load in loads:
        load.start()
    middle = pl.ds(width, cells)
    partner = there(tile, 1 - chan)
    dy_copies = [
        remote(de.at[0, p, :, middle], de.at[1, p, :, middle], dy_send.at[p], dy_recv.at[p], partner)
        for p in range(ZP)
    ]
    for p in range(ZP):
        loads[p].wait()
        de[0, p, :, width : width + cells] = dy_ref[:, p].reshape(own, cells)
        if p == 0:
            expected = 1 + jnp.where(has_above, 1, 0) + jnp.where(has_below, 1, 0)
            pl.semaphore_wait(barrier, expected)
        dy_copies[p].start()
    loads[ZP].wait()
    for p in range(ZP + 2):
        xe[p, :, width : width + cells] = x_ref[:, p].reshape(own, cells)

    @pl.when(tile == 0)
    def _():
        xe[:, :, 0:width] = jnp.zeros((ZP + 2, own, width), bf16)
        de[:, :, :, 0:width] = jnp.zeros((2, ZP, own, width), bf16)

    @pl.when(tile == tiles - 1)
    def _():
        xe[:, :, cells + width : tall] = jnp.zeros((ZP + 2, own, width), bf16)
        de[:, :, :, cells + width : tall] = jnp.zeros((2, ZP, own, width), bf16)

    top, bottom = pl.ds(width, width), pl.ds(cells, width)
    rim_top, rim_bottom = pl.ds(0, width), pl.ds(cells + width, width)

    def rim_copies(to, src_lanes, dst_lanes, at):
        return [
            remote(xe.at[:, :, src_lanes], xe.at[:, :, dst_lanes],
                   rim_send.at[at], rim_recv.at[at], there(to, chan)),
            remote(de.at[0, :, :, src_lanes], de.at[0, :, :, dst_lanes],
                   rim_send.at[at + 1], rim_recv.at[at + 1], there(to, chan)),
        ]

    def downward():
        return rim_copies(tile + 1, bottom, rim_top, 0)

    def upward():
        return rim_copies(tile - 1, top, rim_bottom, 2)

    def far_down():
        return remote(de.at[1, :, :, bottom], de.at[1, :, :, rim_top],
                      far_send.at[0], far_recv.at[0], there(tile + 1, chan))

    def far_up():
        return remote(de.at[1, :, :, top], de.at[1, :, :, rim_bottom],
                      far_send.at[1], far_recv.at[1], there(tile - 1, chan))

    @pl.when(has_below)
    def _():
        for copy in downward():
            copy.start()

    @pl.when(has_above)
    def _():
        for copy in upward():
            copy.start()

    def tell(k):
        step = 2**k

        @pl.when(tile >= step)
        def _():
            pl.semaphore_signal(entered.at[k], inc=1, device_id=there(tile - step, chan),
                                device_id_type=pl.DeviceIdType.MESH)

        @pl.when(tile < tiles - step)
        def _():
            pl.semaphore_signal(entered.at[k], inc=1, device_id=there(tile + step, chan),
                                device_id_type=pl.DeviceIdType.MESH)

    def hear(k):
        step = 2**k
        pl.semaphore_wait(
            entered.at[k], jnp.where(tile >= step, 1, 0) + jnp.where(tile < tiles - step, 1, 0)
        )

    rounds = (tiles - 1).bit_length()
    tell(0)

    loads[ZP + 1].wait()
    whole = w_ref[...].astype(f32)
    swapped = jnp.concatenate([whole[:, own:], whole[:, :own]], axis=1)
    ordered = jnp.where(chan == 0, whole, swapped)
    for kz in range(3):
        wout[(2 - kz) * every : (3 - kz) * every, :] = (
            ordered[kz * taps : (kz + 1) * taps].T.astype(bf16)
        )
    ordered = ordered.astype(bf16)
    for kz in range(3):
        for r in range(9):
            at = (kz * 9 + 8 - r) * own
            for h in range(2):
                win[h, kz * own : (kz + 1) * own, r * own : (r + 1) * own] = (
                    ordered[at : at + own, h * own : (h + 1) * own]
                )


    @pl.when(has_above)
    def _():
        for copy in downward():
            copy.wait_recv()

    @pl.when(has_below)
    def _():
        for copy in upward():
            copy.wait_recv()

    part_copies = [
        remote(coded.at[z], incoming.at[z], part_send.at[z], part_recv.at[z], partner)
        for z in range(ZP)
    ]
    scale_copies = [
        remote(scale_out.at[z], scale_in.at[z], scale_send.at[z], scale_recv.at[z], partner)
        for z in range(ZP)
    ]
    diag = diagonal(own)
    chunk = 2 * width

    def encode(z):
        lanes = jnp.zeros((own, 128), f32)
        for at in range(0, cells, 128):
            lanes = jnp.maximum(lanes, jnp.abs(both[z, own:every, at : at + 128]))
        largest = jnp.maximum(jnp.max(lanes, axis=1, keepdims=True), 1e-30)
        spread = jnp.sum(jnp.where(diag, largest, 0.0), axis=0, keepdims=True)
        scale_out[z] = spread
        inverse = 1.0 / largest
        for at in range(0, cells, chunk):
            coded[z, :, at : at + chunk] = row_codes(both[z, own:every, at : at + chunk], inverse)

    def build(value, target, at):
        copies = tap_copies(value, width)
        for ky in range(3):
            for kx in range(3):
                row = at + (3 * ky + kx) * own
                target[row : row + own, :] = copies[kx][:, ky * width : ky * width + cells]

    def planes_of(p):
        return max(0, p - 2), min(ZP - 1, p)

    for p in range(ZP + 2):
        build(xe[p], x9, p * taps)
        first, last = planes_of(p)
        low = (first - p + 2) * every
        product = jnp.dot(
            wout[low : low + (last - first + 1) * every, :],
            x9[p * taps : (p + 1) * taps, :],
            preferred_element_type=f32,
        )
        for z in range(first, last + 1):
            block = product[(z - first) * every : (z - first + 1) * every]
            if z == p:
                both[z] = block
            else:
                both[z] += block
        if p >= 2:
            encode(p - 2)
        if p in (1, 4) and p // 3 + 1 < rounds:
            hear(p // 3)
            tell(p // 3 + 1)

    def kernel_terms(h):
        for p in range(ZP + 2):
            first, last = planes_of(p)
            count = last - first + 1
            if h == 1 and p == 0:
                for copy in dy_copies[: ZP - 1]:
                    copy.wait_recv()
            if h == 1 and p == ZP - 1:
                dy_copies[p].wait_recv()

                @pl.when(has_below)
                def _():
                    far_down().start()

                @pl.when(has_above)
                def _():
                    far_up().start()

            value = lax.dot_general(
                de[h, first : last + 1, :, width : width + cells].reshape(count * own, cells),
                x9[p * taps : (p + 1) * taps, :],
                (((1,), (1,)), ((), ())),
                preferred_element_type=f32,
            )
            low = (first - p + 2) * own
            if p == 0:
                sums[h] = jnp.zeros_like(sums[h])
            sums[h, low : low + count * own, 0:taps] += value
        for q in range(3):
            terms[h, q * 3 * own : (q + 1) * 3 * own, :] = sums[h, :, q * 128 : (q + 1) * 128]
        rest = sums[h, :, 384:512]
        lane = lax.broadcasted_iota(jnp.int32, (own, 128), 1)
        packed = jnp.where(lane < own, rest[0:own], pltpu.roll(rest[own : 2 * own], own, 1))
        terms[h, 9 * own : 10 * own, :] = packed
        lane = lax.broadcasted_iota(jnp.int32, (own // 2, 128), 1)
        lower, upper = rest[2 * own : 2 * own + own // 2], rest[2 * own + own // 2 :]
        packed = jnp.where(lane < own, lower, pltpu.roll(upper, own, 1))
        terms[h, 10 * own : 10 * own + own // 2, :] = packed
        left = terms.shape[1] - (10 * own + own // 2)
        terms[h, 10 * own + own // 2 :, :] = jnp.zeros((left, 128), f32)

    keep_at = pl.multiple_of(core * half_rows, 8)
    give_at = pl.multiple_of((1 - core) * half_rows, 8)
    keep, give = pl.ds(keep_at, half_rows), pl.ds(give_at, half_rows)
    neighbour = there(chip * 2 + 1 - core, chan)

    def piece_of(index):
        return pl.ds(pl.multiple_of(keep_at + index * piece, 8), piece)

    pair_copies = [
        remote(terms.at[h, give, :], pair_in.at[h], pair_send.at[h], pair_recv.at[h], neighbour)
        for h in range(2)
    ]

    def chip_copy(h, d):
        to = (chip + d) % chips
        return remote(terms.at[h, piece_of(to), :], chip_in.at[h, d - 1],
                      chip_send.at[h, d - 1], chip_recv.at[h, d - 1], there(to * 2 + core, chan))

    def last_copy(h, d):
        to = (chip + d) % chips
        return remote(final.at[h, piece_of(chip), :], final.at[h, piece_of(chip), :],
                      last_send.at[h, d - 1], last_recv.at[h, d - 1], there(to * 2 + core, chan))

    def last_arrival(h, d):
        source = (chip + chips - d) % chips
        return remote(final.at[h, piece_of(source), :], final.at[h, piece_of(source), :],
                      last_send.at[h, d - 1], last_recv.at[h, d - 1],
                      there(source * 2 + core, chan))

    def back_copy(h):
        return remote(final.at[h, keep, :], final.at[h, keep, :],
                      back_send.at[h], back_recv.at[h], neighbour)

    def back_arrival(h):
        return remote(final.at[h, give, :], final.at[h, give, :],
                      back_send.at[h], back_recv.at[h], neighbour)

    def to_chips(h):
        pair_copies[h].wait_recv()
        terms[h, keep, :] += pair_in[h]
        for d in range(1, chips):
            chip_copy(h, d).start()

    def from_chips(h):
        total = terms[h, piece_of(chip), :]
        for d in range(1, chips):
            chip_copy(h, d).wait_recv()
            total += chip_in[h, d - 1]
        final[h, piece_of(chip), :] = total * scale
        for d in range(1, chips):
            last_copy(h, d).start()

    def to_pair(h):
        for d in range(1, chips):
            last_arrival(h, d).wait_recv()
        back_copy(h).start()

    def backward(h, p):
        build(de[h, p], d9.at[p % 2], 0)
        product = jnp.dot(win[h], d9[p % 2], preferred_element_type=f32)
        for kz in range(3):
            block = product[kz * own : (kz + 1) * own]
            if h == 0 and (p == 0 or kz == 2):
                acc[p + kz] = block
            else:
                acc[p + kz] += block

    kernel_terms(0)
    pair_copies[0].start()
    for k in range(2, min(3, rounds)):
        hear(k)
        if k + 1 < rounds:
            tell(k + 1)
    for p in range(ZP):
        backward(0, p)
    for copy in dy_copies:
        copy.wait_send()
    for z in range(ZP):
        scale_copies[z].start()
        part_copies[z].start()
    for k in range(3, rounds):
        hear(k)
        if k + 1 < rounds:
            tell(k + 1)
    to_chips(0)

    kernel_terms(1)
    pair_copies[1].start()
    from_chips(0)

    @pl.when(has_above)
    def _():
        far_down().wait_recv()

    @pl.when(has_below)
    def _():
        far_up().wait_recv()

    def finish(s):
        ingrad_ref[:, s] = acc[s].reshape(own, height, width).astype(bf16)

    to_chips(1)
    backward(1, 0)
    finish(0)
    for p in range(1, ZP):
        backward(1, p)
        finish(p)
    finish(ZP)
    finish(ZP + 1)
    to_pair(0)

    def decode(z):
        scale_copies[z].wait_recv()
        part_copies[z].wait_recv()
        row = jnp.broadcast_to(scale_in[z], (own, 128))
        largest = jnp.sum(jnp.where(diag, row, 0.0), axis=1, keepdims=True)
        for at in range(0, cells, chunk):
            total = both[z, 0:own, at : at + chunk] + row_values(
                incoming[z, :, at : at + chunk], largest
            )
            lines = slice(at // width, (at + chunk) // width)
            out_ref[:, z, lines] = total.reshape(own, chunk // width, width).astype(bf16)

    def turned(h):
        back_arrival(h).wait_recv()
        rows = [final[h, q * 3 * own : (q + 1) * 3 * own, :] for q in range(3)]
        one = final[h, 9 * own : 10 * own, :]
        two = final[h, 10 * own : 10 * own + own // 2, :]
        rest = jnp.concatenate(
            [one, pltpu.roll(one, 128 - own, 1), two, pltpu.roll(two, 128 - own, 1)], axis=0
        )
        half = jnp.concatenate(rows + [rest], axis=1)
        return [half[(2 - kz) * own : (3 - kz) * own].T[:taps] for kz in range(3)]

    from_chips(1)
    decode(0)
    mines = turned(0)
    decode(1)
    to_pair(1)
    decode(2)

    others = turned(1)
    for kz in range(3):
        mine, other = mines[kz], others[kz]
        wgrad_ref[kz * taps : (kz + 1) * taps, :] = jnp.where(
            chan == 0,
            jnp.concatenate([mine, other], axis=1),
            jnp.concatenate([other, mine], axis=1),
        )
    decode(ZP - 1)

    @pl.when(has_below)
    def _():
        for copy in downward() + [far_down()]:
            copy.wait_send()

    @pl.when(has_above)
    def _():
        for copy in upward() + [far_up()]:
            copy.wait_send()

    for copy in part_copies + scale_copies + pair_copies:
        copy.wait_send()
    for h in range(2):
        for d in range(1, chips):
            chip_copy(h, d).wait_send()
            last_copy(h, d).wait_send()
        back_copy(h).wait_send()


def write_kernel(a_ref, b_ref, c_ref, a_out, b_out, c_out, sems):
    copies = [
        pltpu.make_async_copy(source, target, sems.at[k])
        for k, (source, target) in enumerate(((a_ref, a_out), (b_ref, b_out), (c_ref, c_out)))
    ]
    for copy in copies:
        copy.start()
    for copy in copies:
        copy.wait()


def fused_device(x_slab, weights, cotangent):
    every, own = weights.shape[0], weights.shape[1]
    height, width = x_slab.shape[3], x_slab.shape[4]
    cells = height * width
    tall = cells + 2 * width
    tiles = lax.axis_size("tile")
    chips = tiles // 2
    w_taps = weights.transpose(2, 1, 0).reshape(27 * own, every)
    taps = 9 * own
    rows = -(-(10 * own + own // 2) // (16 * chips)) * (16 * chips)
    scale = 1.0 / math.sqrt(ZP * cells * tiles)
    vmem = pl.BlockSpec(memory_space=pltpu.VMEM)
    dma = pltpu.SemaphoreType.DMA
    bf16, f32 = jnp.bfloat16, jnp.float32
    hbm = pl.BlockSpec(memory_space=pl.ANY)
    shapes = (
        ((own, ZP, height, width), bf16),
        ((own, ZP + 2, height, width), bf16),
        ((27 * own, every), f32),
    )
    held = pl.pallas_call(
        functools.partial(fused_kernel, (own, height, width, tiles, scale)),
        out_shape=tuple(pltpu.VMEM(*shape) for shape in shapes),
        in_specs=[hbm] * 3,
        out_specs=(vmem,) * 3,
        scratch_shapes=[
            pltpu.VMEM((own, ZP + 2, height, width), bf16),
            pltpu.VMEM((own, ZP, height, width), bf16),
            pltpu.VMEM((27 * own, every), bf16),
            dma((ZP + 2,)),
            pltpu.SemaphoreType.REGULAR(((tiles - 1).bit_length(),)),
            pltpu.VMEM((ZP + 2, own, tall), bf16),
            pltpu.VMEM((2, ZP, own, tall), bf16),
            pltpu.VMEM(((ZP + 2) * taps, cells), bf16),
            pltpu.VMEM((2, taps, cells), bf16),
            pltpu.VMEM((ZP + 2, own, cells), f32),
            pltpu.VMEM((3 * every, taps), bf16),
            pltpu.VMEM((2, 3 * own, taps), bf16),
            pltpu.VMEM((ZP, every, cells), f32),
            pltpu.VMEM((ZP, own, cells), bf16),
            pltpu.VMEM((ZP, own, cells), bf16),
            pltpu.VMEM((ZP, 1, 128), f32),
            pltpu.VMEM((ZP, 1, 128), f32),
            pltpu.VMEM((2, 3 * own, 512), f32),
            pltpu.VMEM((2, rows, 128), f32),
            pltpu.VMEM((2, rows // 2, 128), f32),
            pltpu.VMEM((2, chips - 1, rows // tiles, 128), f32),
            pltpu.VMEM((2, rows, 128), f32),
            dma((4,)),
            dma((4,)),
            dma((2,)),
            dma((2,)),
            dma((ZP,)),
            dma((ZP,)),
            dma((ZP,)),
            dma((ZP,)),
            dma((ZP,)),
            dma((ZP,)),
            dma((2,)),
            dma((2,)),
            dma((2, chips - 1)),
            dma((2, chips - 1)),
            dma((2, chips - 1)),
            dma((2, chips - 1)),
            dma((2,)),
            dma((2,)),
        ],
        compiler_params=pltpu.CompilerParams(
            vmem_limit_bytes=58 * 1024 * 1024, collective_id=0, has_side_effects=True
        ),
    )(x_slab[0], cotangent[0], w_taps)
    out_flat, in_flat, terms = pl.pallas_call(
        write_kernel,
        out_shape=tuple(jax.ShapeDtypeStruct(*shape) for shape in shapes),
        in_specs=[hbm] * 3,
        out_specs=(hbm,) * 3,
        scratch_shapes=[dma((3,))],
        compiler_params=pltpu.CompilerParams(vmem_limit_bytes=1024 * 1024),
    )(*(pltpu.with_memory_space_constraint(value, pltpu.VMEM) for value in held))
    weight_grad = terms.reshape(27, own, every).transpose(2, 1, 0)
    return (out_flat[None], in_flat[None], weight_grad)


def solution(mesh):
    in_specs = (
        P("tile", "chan", None, None, None),
        P(None, "chan", None),
        P("tile", "chan", None, None, None),
    )
    out_specs = (
        P("tile", "chan", None, None, None),
        P("tile", "chan", None, None, None),
        P(None, "chan", None),
    )
    fused = mesh.shape["chan"] == 2 and mesh.shape["tile"] == 16
    return jax.shard_map(
        fused_device if fused else per_device, mesh=mesh, in_specs=in_specs, out_specs=out_specs, check_vma=False
    )
```

```python
import functools
import math

import jax
import jax.numpy as jnp
from jax import lax
from jax.experimental import pallas as pl
from jax.experimental.pallas import tpu as pltpu
from jax.sharding import PartitionSpec as P

ZP = 4


def shifted(value, axis, steps):
    count = lax.axis_size(axis)
    initial, last = (max(0, -steps), min(count, count - steps))
    return lax.ppermute(value, axis, [(source, source + steps) for source in range(initial, last)])


def with_rims(cells, width):
    above = shifted(cells[:, :, -width:], "tile", 1)
    below = shifted(cells[:, :, :width], "tile", -1)
    return jnp.concatenate([above, cells, below], axis=-1)


def tap_copies(tall, width):
    wide = tall.astype(jnp.float32)
    lanes = wide.shape[1]
    col = lax.broadcasted_iota(jnp.int32, wide.shape, 1) % width
    left = jnp.where(col == 0, 0.0, pltpu.roll(wide, 1, 1)).astype(jnp.bfloat16)
    right = jnp.where(col == width - 1, 0.0, pltpu.roll(wide, lanes - 1, 1)).astype(jnp.bfloat16)
    return left, tall, right


def conv_kernel(
    dims, xe_ref, de_ref, wout_ref, win_ref, part_ref, ingrad_ref, wgrad_ref, x9, d9, acc
):
    own, every, height, width = dims
    cells = height * width
    chunk = 2 * width

    def build_x(p, carry):
        copies = tap_copies(xe_ref[p], width)
        for ky in range(3):
            for kx in range(3):
                at = pl.multiple_of(p * (9 * own) + (3 * ky + kx) * own, 16)
                x9[pl.ds(at, own), :] = copies[kx][:, ky * width : ky * width + cells]
        return carry

    lax.fori_loop(0, ZP + 2, build_x, 0)

    def forward(step, carry):
        z = step // (cells // chunk)
        at = pl.multiple_of((step % (cells // chunk)) * chunk, chunk)
        rows = pl.ds(pl.multiple_of(z * (9 * own), 16), 27 * own)
        part_ref[z, :, pl.ds(at, chunk)] = jnp.dot(
            wout_ref[...], x9[rows, pl.ds(at, chunk)], preferred_element_type=jnp.float32
        )
        return carry

    lax.fori_loop(0, ZP * (cells // chunk), forward, 0)

    acc[...] = jnp.zeros_like(acc)

    def backward(p, carry):
        copies = tap_copies(de_ref[p], width)
        for ky in range(3):
            for kx in range(3):
                at = (3 * ky + kx) * every
                d9[at : at + every, :] = copies[kx][:, ky * width : ky * width + cells]

        def part(j, inner):
            at = pl.multiple_of(j * chunk, chunk)
            product = jnp.dot(
                win_ref[...], d9[:, pl.ds(at, chunk)], preferred_element_type=jnp.float32
            )
            for kz in range(3):
                acc[p + kz, :, pl.ds(at, chunk)] += product[kz * own : (kz + 1) * own]
            return inner

        return lax.fori_loop(0, cells // chunk, part, carry)

    lax.fori_loop(0, ZP, backward, 0)
    ingrad_ref[...] = acc[...].astype(jnp.bfloat16)

    wgrad_ref[...] = jnp.zeros_like(wgrad_ref)

    def kernel_terms(step, carry):
        z, kz = step // 3, step % 3
        rows = pl.ds(pl.multiple_of((z + kz) * (9 * own), 16), 9 * own)
        wgrad_ref[kz] += lax.dot_general(
            de_ref[z, :, width : width + cells],
            x9[rows, :],
            (((1,), (1,)), ((), ())),
            preferred_element_type=jnp.float32,
        )
        return carry

    lax.fori_loop(0, ZP * 3, kernel_terms, 0)


def per_device(x_slab, weights, cotangent):
    every, own_real = weights.shape[0], weights.shape[1]
    own = -(-own_real // 16) * 16
    height, width = x_slab.shape[3], x_slab.shape[4]
    cells = height * width
    spare = own - own_real
    flat_x = x_slab[0].transpose(1, 0, 2, 3).reshape(ZP + 2, own_real, cells)
    flat_dy = cotangent[0].transpose(1, 0, 2, 3).reshape(ZP, own_real, cells)
    dy_all = lax.all_gather(flat_dy, "chan", axis=1, tiled=True)
    x_rims = with_rims(flat_x, width)
    d_rims = with_rims(dy_all, width)
    if spare:
        x_rims = jnp.pad(x_rims, ((0, 0), (0, spare), (0, 0)))
        weights = jnp.pad(weights, ((0, 0), (0, spare), (0, 0)))
    w_out = weights.transpose(0, 2, 1).reshape(every, 27 * own)
    w_in = (
        weights.reshape(every, own, 3, 9)[:, :, :, ::-1]
        .transpose(2, 1, 3, 0)
        .reshape(3 * own, 9 * every)
    )
    vmem = pl.BlockSpec(memory_space=pltpu.VMEM)
    part, in_flat, terms = pl.pallas_call(
        functools.partial(conv_kernel, (own, every, height, width)),
        out_shape=(
            jax.ShapeDtypeStruct((ZP, every, cells), jnp.float32),
            jax.ShapeDtypeStruct((ZP + 2, own, cells), jnp.bfloat16),
            jax.ShapeDtypeStruct((3, every, 9 * own), jnp.float32),
        ),
        in_specs=[vmem] * 4,
        out_specs=(vmem,) * 3,
        scratch_shapes=[
            pltpu.VMEM(((ZP + 2) * 9 * own, cells), jnp.bfloat16),
            pltpu.VMEM((9 * every, cells), jnp.bfloat16),
            pltpu.VMEM((ZP + 2, own, cells), jnp.float32),
        ],
        compiler_params=pltpu.CompilerParams(vmem_limit_bytes=48 * 1024 * 1024),
    )(x_rims, d_rims, w_out, w_in)
    total = lax.psum_scatter(part, "chan", scatter_dimension=1, tiled=True)
    out_field = (
        total.astype(jnp.bfloat16)
        .reshape(ZP, own_real, height, width)
        .transpose(1, 0, 2, 3)[None]
    )
    in_grad = (
        in_flat[:, :own_real].reshape(ZP + 2, own_real, height, width).transpose(1, 0, 2, 3)[None]
    )
    scale = 1.0 / math.sqrt(ZP * cells * lax.axis_size("tile"))
    summed = lax.psum(terms, "tile") * scale
    weight_grad = (
        summed.reshape(3, every, 9, own)[..., :own_real]
        .transpose(1, 3, 0, 2)
        .reshape(every, own_real, 27)
    )
    return (out_field, in_grad, weight_grad)


LEVELS = 250.0
BEND = 3.0


def row_codes(value, inverse):
    ratio = jnp.abs(value) * inverse
    bent = ratio * (1.0 + BEND) / (1.0 + BEND * ratio)
    size = jnp.exp2(bent * LEVELS - 0.5 * LEVELS)
    return jnp.where(value < 0.0, -size, size).astype(jnp.bfloat16)


def row_values(codes, largest):
    wide = codes.astype(jnp.float32)
    bent = jnp.log2(jnp.abs(wide)) * (1.0 / LEVELS) + 0.5
    size = bent * largest / ((1.0 + BEND) - BEND * bent)
    return jnp.where(wide < 0.0, -size, size)


def diagonal(count):
    shape = (count, 128)
    return lax.broadcasted_iota(jnp.int32, shape, 0) == lax.broadcasted_iota(jnp.int32, shape, 1)


def fused_kernel(
    dims,
    x_hbm,
    dy_hbm,
    w_hbm,
    out_ref,
    ingrad_ref,
    wgrad_ref,
    x_ref,
    dy_ref,
    w_ref,
    load_sem,
    entered,
    xe,
    de,
    x9,
    d9,
    acc,
    wout,
    win,
    both,
    coded,
    incoming,
    scale_out,
    scale_in,
    sums,
    terms,
    pair_in,
    chip_in,
    final,
    rim_send,
    rim_recv,
    far_send,
    far_recv,
    dy_send,
    dy_recv,
    part_send,
    part_recv,
    scale_send,
    scale_recv,
    pair_send,
    pair_recv,
    chip_send,
    chip_recv,
    last_send,
    last_recv,
    back_send,
    back_recv,
):
    own, height, width, tiles, scale = dims
    every = 2 * own
    taps = 9 * own
    cells = height * width
    tall = cells + 2 * width
    tile, chan = lax.axis_index("tile"), lax.axis_index("chan")
    core, chip, chips = tile % 2, tile // 2, tiles // 2
    half_rows = terms.shape[1] // 2
    piece = half_rows // chips
    f32, bf16 = jnp.float32, jnp.bfloat16

    def there(t, c):
        return {"tile": t, "chan": c}

    def remote(src, dst, send, recv, to):
        return pltpu.make_async_remote_copy(
            src_ref=src,
            dst_ref=dst,
            send_sem=send,
            recv_sem=recv,
            device_id=to,
            device_id_type=pl.DeviceIdType.MESH,
        )

    barrier = pltpu.get_barrier_semaphore()

    def greet(to):
        pl.semaphore_signal(barrier, inc=1, device_id=to, device_id_type=pl.DeviceIdType.MESH)

    has_above, has_below = tile > 0, tile < tiles - 1
    greet(there(tile, 1 - chan))

    @pl.when(has_above)
    def _():
        greet(there(tile - 1, chan))

    @pl.when(has_below)
    def _():
        greet(there(tile + 1, chan))

    loads = [
        pltpu.make_async_copy(source, target, load_sem.at[k])
        for k, (source, target) in enumerate(
            [(dy_hbm.at[:, p], dy_ref.at[:, p]) for p in range(ZP)]
            + [(x_hbm, x_ref), (w_hbm, w_ref)]
        )
    ]
    for load in loads:
        load.start()
    middle = pl.ds(width, cells)
    partner = there(tile, 1 - chan)
    dy_copies = [
        remote(de.at[0, p, :, middle], de.at[1, p, :, middle], dy_send.at[p], dy_recv.at[p], partner)
        for p in range(ZP)
    ]
    for p in range(ZP):
        loads[p].wait()
        de[0, p, :, width : width + cells] = dy_ref[:, p].reshape(own, cells)
        if p == 0:
            expected = 1 + jnp.where(has_above, 1, 0) + jnp.where(has_below, 1, 0)
            pl.semaphore_wait(barrier, expected)
        dy_copies[p].start()
    loads[ZP].wait()
    for p in range(ZP + 2):
        xe[p, :, width : width + cells] = x_ref[:, p].reshape(own, cells)

    @pl.when(tile == 0)
    def _():
        xe[:, :, 0:width] = jnp.zeros((ZP + 2, own, width), bf16)
        de[:, :, :, 0:width] = jnp.zeros((2, ZP, own, width), bf16)

    @pl.when(tile == tiles - 1)
    def _():
        xe[:, :, cells + width : tall] = jnp.zeros((ZP + 2, own, width), bf16)
        de[:, :, :, cells + width : tall] = jnp.zeros((2, ZP, own, width), bf16)

    top, bottom = pl.ds(width, width), pl.ds(cells, width)
    rim_top, rim_bottom = pl.ds(0, width), pl.ds(cells + width, width)

    def rim_copies(to, src_lanes, dst_lanes, at):
        return [
            remote(xe.at[:, :, src_lanes], xe.at[:, :, dst_lanes],
                   rim_send.at[at], rim_recv.at[at], there(to, chan)),
            remote(de.at[0, :, :, src_lanes], de.at[0, :, :, dst_lanes],
                   rim_send.at[at + 1], rim_recv.at[at + 1], there(to, chan)),
        ]

    def downward():
        return rim_copies(tile + 1, bottom, rim_top, 0)

    def upward():
        return rim_copies(tile - 1, top, rim_bottom, 2)

    def far_down():
        return remote(de.at[1, :, :, bottom], de.at[1, :, :, rim_top],
                      far_send.at[0], far_recv.at[0], there(tile + 1, chan))

    def far_up():
        return remote(de.at[1, :, :, top], de.at[1, :, :, rim_bottom],
                      far_send.at[1], far_recv.at[1], there(tile - 1, chan))

    @pl.when(has_below)
    def _():
        for copy in downward():
            copy.start()

    @pl.when(has_above)
    def _():
        for copy in upward():
            copy.start()

    def tell(k):
        step = 2**k

        @pl.when(tile >= step)
        def _():
            pl.semaphore_signal(entered.at[k], inc=1, device_id=there(tile - step, chan),
                                device_id_type=pl.DeviceIdType.MESH)

        @pl.when(tile < tiles - step)
        def _():
            pl.semaphore_signal(entered.at[k], inc=1, device_id=there(tile + step, chan),
                                device_id_type=pl.DeviceIdType.MESH)

    def hear(k):
        step = 2**k
        pl.semaphore_wait(
            entered.at[k], jnp.where(tile >= step, 1, 0) + jnp.where(tile < tiles - step, 1, 0)
        )

    rounds = (tiles - 1).bit_length()
    tell(0)

    loads[ZP + 1].wait()
    whole = w_ref[...].astype(f32)
    swapped = jnp.concatenate([whole[:, own:], whole[:, :own]], axis=1)
    ordered = jnp.where(chan == 0, whole, swapped)
    for kz in range(3):
        wout[(2 - kz) * every : (3 - kz) * every, :] = (
            ordered[kz * taps : (kz + 1) * taps].T.astype(bf16)
        )
    ordered = ordered.astype(bf16)
    for kz in range(3):
        for r in range(9):
            at = (kz * 9 + 8 - r) * own
            for h in range(2):
                win[h, kz * own : (kz + 1) * own, r * own : (r + 1) * own] = (
                    ordered[at : at + own, h * own : (h + 1) * own]
                )


    @pl.when(has_above)
    def _():
        for copy in downward():
            copy.wait_recv()

    @pl.when(has_below)
    def _():
        for copy in upward():
            copy.wait_recv()

    part_copies = [
        remote(coded.at[z], incoming.at[z], part_send.at[z], part_recv.at[z], partner)
        for z in range(ZP)
    ]
    scale_copies = [
        remote(scale_out.at[z], scale_in.at[z], scale_send.at[z], scale_recv.at[z], partner)
        for z in range(ZP)
    ]
    diag = diagonal(own)
    chunk = 2 * width

    def encode(z):
        lanes = jnp.zeros((own, 128), f32)
        for at in range(0, cells, 128):
            lanes = jnp.maximum(lanes, jnp.abs(both[z, own:every, at : at + 128]))
        largest = jnp.maximum(jnp.max(lanes, axis=1, keepdims=True), 1e-30)
        spread = jnp.sum(jnp.where(diag, largest, 0.0), axis=0, keepdims=True)
        scale_out[z] = spread
        inverse = 1.0 / largest
        for at in range(0, cells, chunk):
            coded[z, :, at : at + chunk] = row_codes(both[z, own:every, at : at + chunk], inverse)

    def build(value, target, at):
        copies = tap_copies(value, width)
        for ky in range(3):
            for kx in range(3):
                row = at + (3 * ky + kx) * own
                target[row : row + own, :] = copies[kx][:, ky * width : ky * width + cells]

    def planes_of(p):
        return max(0, p - 2), min(ZP - 1, p)

    for p in range(ZP + 2):
        build(xe[p], x9, p * taps)
        first, last = planes_of(p)
        low = (first - p + 2) * every
        product = jnp.dot(
            wout[low : low + (last - first + 1) * every, :],
            x9[p * taps : (p + 1) * taps, :],
            preferred_element_type=f32,
        )
        for z in range(first, last + 1):
            block = product[(z - first) * every : (z - first + 1) * every]
            if z == p:
                both[z] = block
            else:
                both[z] += block
        if p >= 2:
            encode(p - 2)
        if p in (1, 4) and p // 3 + 1 < rounds:
            hear(p // 3)
            tell(p // 3 + 1)

    def kernel_terms(h):
        for p in range(ZP + 2):
            first, last = planes_of(p)
            count = last - first + 1
            if h == 1 and p == 0:
                for copy in dy_copies[: ZP - 1]:
                    copy.wait_recv()
            if h == 1 and p == ZP - 1:
                dy_copies[p].wait_recv()

                @pl.when(has_below)
                def _():
                    far_down().start()

                @pl.when(has_above)
                def _():
                    far_up().start()

            value = lax.dot_general(
                de[h, first : last + 1, :, width : width + cells].reshape(count * own, cells),
                x9[p * taps : (p + 1) * taps, :],
                (((1,), (1,)), ((), ())),
                preferred_element_type=f32,
            )
            low = (first - p + 2) * own
            if p == 0:
                sums[h] = jnp.zeros_like(sums[h])
            sums[h, low : low + count * own, 0:taps] += value
        for q in range(3):
            terms[h, q * 3 * own : (q + 1) * 3 * own, :] = sums[h, :, q * 128 : (q + 1) * 128]
        rest = sums[h, :, 384:512]
        lane = lax.broadcasted_iota(jnp.int32, (own, 128), 1)
        packed = jnp.where(lane < own, rest[0:own], pltpu.roll(rest[own : 2 * own], own, 1))
        terms[h, 9 * own : 10 * own, :] = packed
        lane = lax.broadcasted_iota(jnp.int32, (own // 2, 128), 1)
        lower, upper = rest[2 * own : 2 * own + own // 2], rest[2 * own + own // 2 :]
        packed = jnp.where(lane < own, lower, pltpu.roll(upper, own, 1))
        terms[h, 10 * own : 10 * own + own // 2, :] = packed
        left = terms.shape[1] - (10 * own + own // 2)
        terms[h, 10 * own + own // 2 :, :] = jnp.zeros((left, 128), f32)

    keep_at = pl.multiple_of(core * half_rows, 8)
    give_at = pl.multiple_of((1 - core) * half_rows, 8)
    keep, give = pl.ds(keep_at, half_rows), pl.ds(give_at, half_rows)
    neighbour = there(chip * 2 + 1 - core, chan)

    def piece_of(index):
        return pl.ds(pl.multiple_of(keep_at + index * piece, 8), piece)

    pair_copies = [
        remote(terms.at[h, give, :], pair_in.at[h], pair_send.at[h], pair_recv.at[h], neighbour)
        for h in range(2)
    ]

    def chip_copy(h, d):
        to = (chip + d) % chips
        return remote(terms.at[h, piece_of(to), :], chip_in.at[h, d - 1],
                      chip_send.at[h, d - 1], chip_recv.at[h, d - 1], there(to * 2 + core, chan))

    def last_copy(h, d):
        to = (chip + d) % chips
        return remote(final.at[h, piece_of(chip), :], final.at[h, piece_of(chip), :],
                      last_send.at[h, d - 1], last_recv.at[h, d - 1], there(to * 2 + core, chan))

    def last_arrival(h, d):
        source = (chip + chips - d) % chips
        return remote(final.at[h, piece_of(source), :], final.at[h, piece_of(source), :],
                      last_send.at[h, d - 1], last_recv.at[h, d - 1],
                      there(source * 2 + core, chan))

    def back_copy(h):
        return remote(final.at[h, keep, :], final.at[h, keep, :],
                      back_send.at[h], back_recv.at[h], neighbour)

    def back_arrival(h):
        return remote(final.at[h, give, :], final.at[h, give, :],
                      back_send.at[h], back_recv.at[h], neighbour)

    def to_chips(h):
        pair_copies[h].wait_recv()
        terms[h, keep, :] += pair_in[h]
        for d in range(1, chips):
            chip_copy(h, d).start()

    def from_chips(h):
        total = terms[h, piece_of(chip), :]
        for d in range(1, chips):
            chip_copy(h, d).wait_recv()
            total += chip_in[h, d - 1]
        final[h, piece_of(chip), :] = total * scale
        for d in range(1, chips):
            last_copy(h, d).start()

    def to_pair(h):
        for d in range(1, chips):
            last_arrival(h, d).wait_recv()
        back_copy(h).start()

    def backward(h, p):
        build(de[h, p], d9.at[p % 2], 0)
        product = jnp.dot(win[h], d9[p % 2], preferred_element_type=f32)
        for kz in range(3):
            block = product[kz * own : (kz + 1) * own]
            if h == 0 and (p == 0 or kz == 2):
                acc[p + kz] = block
            else:
                acc[p + kz] += block

    kernel_terms(0)
    pair_copies[0].start()
    for k in range(2, min(3, rounds)):
        hear(k)
        if k + 1 < rounds:
            tell(k + 1)
    for p in range(ZP):
        backward(0, p)
    for k in range(3, rounds):
        hear(k)
        if k + 1 < rounds:
            tell(k + 1)
    to_chips(0)

    for copy in dy_copies:
        copy.wait_send()
    for z in range(ZP):
        scale_copies[z].start()
        part_copies[z].start()
    kernel_terms(1)
    pair_copies[1].start()
    from_chips(0)

    @pl.when(has_above)
    def _():
        far_down().wait_recv()

    @pl.when(has_below)
    def _():
        far_up().wait_recv()

    def finish(s):
        ingrad_ref[:, s] = acc[s].reshape(own, height, width).astype(bf16)

    to_chips(1)
    backward(1, 0)
    finish(0)
    for p in range(1, ZP):
        backward(1, p)
        finish(p)
    finish(ZP)
    finish(ZP + 1)
    to_pair(0)

    def decode(z):
        scale_copies[z].wait_recv()
        part_copies[z].wait_recv()
        row = jnp.broadcast_to(scale_in[z], (own, 128))
        largest = jnp.sum(jnp.where(diag, row, 0.0), axis=1, keepdims=True)
        for at in range(0, cells, chunk):
            total = both[z, 0:own, at : at + chunk] + row_values(
                incoming[z, :, at : at + chunk], largest
            )
            lines = slice(at // width, (at + chunk) // width)
            out_ref[:, z, lines] = total.reshape(own, chunk // width, width).astype(bf16)

    def turned(h):
        back_arrival(h).wait_recv()
        rows = [final[h, q * 3 * own : (q + 1) * 3 * own, :] for q in range(3)]
        one = final[h, 9 * own : 10 * own, :]
        two = final[h, 10 * own : 10 * own + own // 2, :]
        rest = jnp.concatenate(
            [one, pltpu.roll(one, 128 - own, 1), two, pltpu.roll(two, 128 - own, 1)], axis=0
        )
        half = jnp.concatenate(rows + [rest], axis=1)
        return [half[(2 - kz) * own : (3 - kz) * own].T[:taps] for kz in range(3)]

    from_chips(1)
    decode(0)
    mines = turned(0)
    decode(1)
    to_pair(1)
    decode(2)

    others = turned(1)
    for kz in range(3):
        mine, other = mines[kz], others[kz]
        wgrad_ref[kz * taps : (kz + 1) * taps, :] = jnp.where(
            chan == 0,
            jnp.concatenate([mine, other], axis=1),
            jnp.concatenate([other, mine], axis=1),
        )
    @pl.when(has_below)
    def _():
        for copy in downward() + [far_down()]:
            copy.wait_send()

    @pl.when(has_above)
    def _():
        for copy in upward() + [far_up()]:
            copy.wait_send()

    for copy in part_copies[: ZP - 1] + scale_copies + pair_copies:
        copy.wait_send()
    for h in range(2):
        for d in range(1, chips):
            chip_copy(h, d).wait_send()
            last_copy(h, d).wait_send()
        back_copy(h).wait_send()
    decode(ZP - 1)
    part_copies[ZP - 1].wait_send()


def write_kernel(a_ref, b_ref, c_ref, a_out, b_out, c_out, sems):
    copies = [
        pltpu.make_async_copy(source, target, sems.at[k])
        for k, (source, target) in enumerate(((a_ref, a_out), (b_ref, b_out), (c_ref, c_out)))
    ]
    for copy in copies:
        copy.start()
    for copy in copies:
        copy.wait()


def fused_device(x_slab, weights, cotangent):
    every, own = weights.shape[0], weights.shape[1]
    height, width = x_slab.shape[3], x_slab.shape[4]
    cells = height * width
    tall = cells + 2 * width
    tiles = lax.axis_size("tile")
    chips = tiles // 2
    w_taps = weights.transpose(2, 1, 0).reshape(27 * own, every)
    taps = 9 * own
    rows = -(-(10 * own + own // 2) // (16 * chips)) * (16 * chips)
    scale = 1.0 / math.sqrt(ZP * cells * tiles)
    vmem = pl.BlockSpec(memory_space=pltpu.VMEM)
    dma = pltpu.SemaphoreType.DMA
    bf16, f32 = jnp.bfloat16, jnp.float32
    hbm = pl.BlockSpec(memory_space=pl.ANY)
    shapes = (
        ((own, ZP, height, width), bf16),
        ((own, ZP + 2, height, width), bf16),
        ((27 * own, every), f32),
    )
    held = pl.pallas_call(
        functools.partial(fused_kernel, (own, height, width, tiles, scale)),
        out_shape=tuple(pltpu.VMEM(*shape) for shape in shapes),
        in_specs=[hbm] * 3,
        out_specs=(vmem,) * 3,
        scratch_shapes=[
            pltpu.VMEM((own, ZP + 2, height, width), bf16),
            pltpu.VMEM((own, ZP, height, width), bf16),
            pltpu.VMEM((27 * own, every), bf16),
            dma((ZP + 2,)),
            pltpu.SemaphoreType.REGULAR(((tiles - 1).bit_length(),)),
            pltpu.VMEM((ZP + 2, own, tall), bf16),
            pltpu.VMEM((2, ZP, own, tall), bf16),
            pltpu.VMEM(((ZP + 2) * taps, cells), bf16),
            pltpu.VMEM((2, taps, cells), bf16),
            pltpu.VMEM((ZP + 2, own, cells), f32),
            pltpu.VMEM((3 * every, taps), bf16),
            pltpu.VMEM((2, 3 * own, taps), bf16),
            pltpu.VMEM((ZP, every, cells), f32),
            pltpu.VMEM((ZP, own, cells), bf16),
            pltpu.VMEM((ZP, own, cells), bf16),
            pltpu.VMEM((ZP, 1, 128), f32),
            pltpu.VMEM((ZP, 1, 128), f32),
            pltpu.VMEM((2, 3 * own, 512), f32),
            pltpu.VMEM((2, rows, 128), f32),
            pltpu.VMEM((2, rows // 2, 128), f32),
            pltpu.VMEM((2, chips - 1, rows // tiles, 128), f32),
            pltpu.VMEM((2, rows, 128), f32),
            dma((4,)),
            dma((4,)),
            dma((2,)),
            dma((2,)),
            dma((ZP,)),
            dma((ZP,)),
            dma((ZP,)),
            dma((ZP,)),
            dma((ZP,)),
            dma((ZP,)),
            dma((2,)),
            dma((2,)),
            dma((2, chips - 1)),
            dma((2, chips - 1)),
            dma((2, chips - 1)),
            dma((2, chips - 1)),
            dma((2,)),
            dma((2,)),
        ],
        compiler_params=pltpu.CompilerParams(
            vmem_limit_bytes=58 * 1024 * 1024, collective_id=0, has_side_effects=True
        ),
    )(x_slab[0], cotangent[0], w_taps)
    out_flat, in_flat, terms = pl.pallas_call(
        write_kernel,
        out_shape=tuple(jax.ShapeDtypeStruct(*shape) for shape in shapes),
        in_specs=[hbm] * 3,
        out_specs=(hbm,) * 3,
        scratch_shapes=[dma((3,))],
        compiler_params=pltpu.CompilerParams(vmem_limit_bytes=1024 * 1024),
    )(*(pltpu.with_memory_space_constraint(value, pltpu.VMEM) for value in held))
    weight_grad = terms.reshape(27, own, every).transpose(2, 1, 0)
    return (out_flat[None], in_flat[None], weight_grad)


def solution(mesh):
    in_specs = (
        P("tile", "chan", None, None, None),
        P(None, "chan", None),
        P("tile", "chan", None, None, None),
    )
    out_specs = (
        P("tile", "chan", None, None, None),
        P("tile", "chan", None, None, None),
        P(None, "chan", None),
    )
    fused = mesh.shape["chan"] == 2 and mesh.shape["tile"] == 16
    return jax.shard_map(
        fused_device if fused else per_device, mesh=mesh, in_specs=in_specs, out_specs=out_specs, check_vma=False
    )
```
